32 devices in a mesh: lon: 4 (over z), lat: 8 (over y, x, core).
Axes of the slice: x: 2, y: 2, z: 4, core: 2. Of those that a mesh axis runs over, the one named last changes fastest.
Arguments:
- tracers: float32 [3, 8, 64, 512], P(None, None, 'lat', 'lon'), may hold values from -6 to 6
- cotangent: float32 [3, 8, 64, 512], P(None, None, 'lat', 'lon'), may hold values from -6 to 6
- east_vel: float32 [8, 64, 512], P(None, 'lat', 'lon'), may hold values from -0.3 to 0.3
- north_vel: float32 [8, 64, 512], P(None, 'lat', 'lon'), may hold values from -0.3 to 0.3
- sea_mask: int32 [64, 512], P('lat', 'lon'), may hold values 0 or 1
- level_count: int32 [64, 512], P('lat', 'lon'), may hold values from 1 to 8
Outputs:
- adj_tracers: float32 [3, 8, 64, 512], P(None, None, 'lat', 'lon')
- adj_east: float32 [8, 64, 512], P(None, 'lat', 'lon')
- adj_north: float32 [8, 64, 512], P(None, 'lat', 'lon')
The draws below stay inside these ranges and needn't reach their ends.
All inputs are finite; a program needn't handle non-finite values. No bound on the sum of `sea_mask` on one device may be relied on, other than what follows from the above.
Results may differ from the reference program's by a relative error of at most 0.00002.
Values sent between devices are 32-bit elements; how exact they have to be, the bound alone decides.
No kernel may reach another device: no remote copies, remote signals or barrier semaphores. Data moves between devices by JAX's collectives and lax.ppermute only.
A program may use at most 64 MiB of HBM per device.

```python
import jax
import jax.numpy as jnp
from jax import lax

TRACERS = 3
LEV = 8
STEPS = 4
NLAT = 64
NLON = 512


def draw_cotangent(key, part):
    shape = (TRACERS, LEV, NLAT, NLON)
    own_key = jax.random.fold_in(key, 101)
    return jnp.clip(jax.random.normal(own_key, shape, jnp.float32), -6.0, 6.0)


def draw_east_vel(key, part):
    shape = (LEV, NLAT, NLON)
    own_key = jax.random.fold_in(key, 202)
    return jax.random.uniform(own_key, shape, jnp.float32, -0.3, 0.3)


def draw_north_vel(key, part):
    shape = (LEV, NLAT, NLON)
    own_key = jax.random.fold_in(key, 303)
    return jax.random.uniform(own_key, shape, jnp.float32, -0.3, 0.3)


def with_ends(drawn, rng, least, top_value):
    place = [jax.random.randint(jax.random.fold_in(rng, axis), (), 0, length) for axis, length in enumerate(drawn.shape)]
    main_axis = drawn.shape.index(max(drawn.shape))
    next_to = place[:main_axis] + [(place[main_axis] + 1) % drawn.shape[main_axis]] + place[main_axis + 1:]
    return drawn.at[tuple(place)].set(least).at[tuple(next_to)].set(top_value)


def shard_levels(rng, extent, shards, low, high):
    gain, own = 1.0, jax.random.fold_in(rng, 6)
    for dim, shards_of in shards:
        heights = jnp.exp(jax.random.uniform(jax.random.fold_in(own, dim), (shards_of,), jnp.float32, low / len(shards), high / len(shards)))
        gain = gain * jnp.repeat(heights, extent[dim] // shards_of).reshape([-1 if axis == dim else 1 for axis in range(len(extent))])
    return gain


def noise(stream_key, shape, deviation, reach, pieces=(), dtype=jnp.bfloat16):
    values = jax.random.normal(stream_key, shape, jnp.float32) * deviation
    if len(pieces) > 0:
        values = shard_levels(stream_key, shape, pieces, -0.22, 0.18) * values
    return jnp.clip(values, min=-reach, max=reach).astype(dtype)


def setup_inputs(seed: int = 0) -> dict:
    streams_of = jax.random.split(jax.random.key(seed), 7)
    return {
        "tracers": noise(streams_of[0], (TRACERS, LEV, NLAT, NLON), 1.0, 6.0, ((2, 8), (3, 4)), jnp.float32),
        "cotangent": draw_cotangent(jax.random.fold_in(streams_of[6], 71), 0),
        "east_vel": draw_east_vel(jax.random.fold_in(streams_of[6], 71), 0),
        "north_vel": draw_north_vel(jax.random.fold_in(streams_of[6], 71), 0),
        "sea_mask": with_ends((jax.random.randint(streams_of[4], (NLAT, NLON), 0, 8) < 7).astype(jnp.int32), jax.random.fold_in(streams_of[4], 1), 0, 1),
        "level_count": with_ends(jax.random.randint(streams_of[5], (NLAT, NLON), 1, LEV + 1), jax.random.fold_in(streams_of[5], 1), 1, LEV).astype(jnp.int32),
    }


horiz_diff = 0.22
vert_diff = 0.05

def advance(tracer, east_field, north_field, wetness):
    row_part = tracer[..., 1:-1, :]
    row_wet = wetness[:, 1:-1, :]
    east_open = row_wet[:, :, :-1] * row_wet[:, :, 1:]
    east_flux = east_open * (east_field[:, 1:-1, :-1] * 0.5 * (row_part[..., :-1] + row_part[..., 1:]) - horiz_diff * (row_part[..., 1:] - row_part[..., :-1]))
    column_part = tracer[..., :, 1:-1]
    column_wet = wetness[:, :, 1:-1]
    north_open = column_wet[:, :-1, :] * column_wet[:, 1:, :]
    north_flux = north_open * (north_field[:, :-1, 1:-1] * 0.5 * (column_part[..., :-1, :] + column_part[..., 1:, :]) - horiz_diff * (column_part[..., 1:, :] - column_part[..., :-1, :]))
    centre = tracer[..., 1:-1, 1:-1]
    centre_wet = wetness[:, 1:-1, 1:-1]
    vertical_open = centre_wet[:-1] * centre_wet[1:]
    vertical_flux = vertical_open * vert_diff * (centre[..., 1:, :, :] - centre[..., :-1, :, :])
    nothing = jnp.zeros_like(centre[..., :1, :, :])
    mixing = jnp.concatenate([vertical_flux, nothing], -3) - jnp.concatenate([nothing, vertical_flux], -3)
    return centre_wet * (centre - (east_flux[..., 1:] - east_flux[..., :-1]) - (north_flux[..., 1:, :] - north_flux[..., :-1, :]) + mixing)

def wet_cells(sea_mask, level_count):
    level_index = lax.broadcasted_iota(jnp.int32, (LEV,) + sea_mask.shape, 0)
    return jnp.where((sea_mask[None] == 1) & (level_index < level_count[None]), 1.0, 0.0).astype(jnp.float32)

def widen(field_in):
    wrapped = jnp.concatenate([field_in[..., -1:], field_in, field_in[..., :1]], -1)
    border = jnp.zeros_like(wrapped[..., :1, :])
    return jnp.concatenate([border, wrapped, border], -2)

def reference(tracers, cotangent, east_vel, north_vel, sea_mask, level_count):
    wide_wet = widen(wet_cells(sea_mask, level_count))

    def forward(initial, east_field, north_field):
        east_wide = widen(east_field)
        north_wide = widen(north_field)
        current = initial
        for repeat in range(STEPS):
            current = jax.checkpoint(advance)(widen(current), east_wide, north_wide, wide_wet)
        return current

    def one_tracer(members):
        initial, sensitivity = members
        ending, pullback = jax.vjp(forward, initial[None], east_vel, north_vel)
        gradients = pullback(sensitivity[None])
        return (gradients[0][0], gradients[1], gradients[2])
    adj_tracers, east_parts, north_parts = lax.map(one_tracer, (tracers, cotangent))
    return (adj_tracers, lax.optimization_barrier(jnp.sum(east_parts, 0)), lax.optimization_barrier(jnp.sum(north_parts, 0)))
```

```python
import jax
import jax.numpy as jnp
from jax import lax
from jax.experimental import pallas as pl
from jax.experimental.pallas import tpu as pltpu
from jax.sharding import PartitionSpec as P

STEPS = 4
HORIZ = 0.22
VERT = 0.05

ROWS = 8
LANES = 128
RIM = 4
SLOT = 16
F32 = jnp.float32
VMEM = 8 << 20


def iota(axis):
    return lax.broadcasted_iota(jnp.int32, (ROWS, LANES), axis)


def lane_roll(x, shift):
    shift %= LANES
    return x if shift == 0 else pltpu.roll(x, shift, 1)


def row_roll(x, shift):
    return pltpu.roll(x, shift % ROWS, 0)


def east(x):
    return lane_roll(x, -1)


def west(x):
    return lane_roll(x, 1)


def north(own, rim, last):
    a, b = row_roll(own, -1), row_roll(rim, -1)
    return jnp.where(last, b, a), jnp.where(last, a, b)


def south(own, rim, first):
    a, b = row_roll(own, 1), row_roll(rim, 1)
    return jnp.where(first, b, a), jnp.where(first, a, b)


def odd_row():
    return lax.rem(lax.axis_index("lat"), 2)


def wet_count(mask, count):
    return jnp.where(mask == 1, count, 0).astype(F32)


def edge_of(planes):
    slot = iota(1) // SLOT
    out = None
    for k, plane in enumerate(planes):
        moved = lane_roll(plane, SLOT * k + SLOT // 2)
        out = moved if out is None else jnp.where(slot == k, moved, out)
    return out


def inside_rows(rim):
    place, total = lax.axis_index("lat"), lax.axis_size("lat")
    sub = iota(0)
    keep = ((sub >= RIM) | (place < total - 1)) & ((sub < RIM) | (place > 0))
    return jnp.where(keep, rim, 0.0)


def pack_kernel(*refs):
    args, here, (pair_a, pair_b, to_west, to_east, edge, sems) = refs[:6], refs[6:12], refs[12:]
    copies = [pltpu.make_async_copy(a, b, sems.at[i]) for i, (a, b) in enumerate(zip(args, here))]
    for copy in copies:
        copy.start()
    for copy in copies:
        copy.wait()
    trac, cot, east_vel, north_vel, mask, count = here
    n_trac, lev = trac.shape[:2]
    upper = (iota(0) // RIM) != odd_row()

    def pair(index, p, q):
        q = row_roll(q, RIM)
        pair_a[index] = jnp.where(upper, p, q)
        pair_b[index] = jnp.where(upper, q, p)

    for t in range(n_trac):
        for k in range(lev):
            pair(t * lev + k, trac[t, k], cot[t, k])
    for k in range(lev):
        pair(n_trac * lev + k, east_vel[k], north_vel[k])
    wet = wet_count(mask[...], count[...])
    pair_a[(n_trac + 1) * lev] = wet
    pair_b[(n_trac + 1) * lev] = wet

    fields = [[trac[t, k] for k in range(lev)] for t in range(n_trac)]
    fields += [[cot[t, k] for k in range(lev)] for t in range(n_trac)]
    fields += [[ref[k] for k in range(lev)] for ref in (east_vel, north_vel)]
    fields += [[wet] * lev]
    quarter = (iota(1) % SLOT) // RIM
    west_out, east_out = {}, {}
    for f, planes in enumerate(fields):
        e = edge_of(planes)
        edge[f] = e
        d, g = divmod(f, SLOT // RIM)
        if f == len(fields) - 1 and g == 0:
            west_out[d] = east_out[d] = e
            continue
        moved = lane_roll(e, RIM * g - 8)
        if g == 0:
            west_out[d] = east_out[d] = moved
        else:
            west_out[d] = jnp.where(quarter == g, moved, west_out[d])
            east_out[d] = jnp.where(quarter == g - 1, moved, east_out[d])
    for d in west_out:
        to_west[d] = west_out[d]
        to_east[d] = east_out[d]


def corner_kernel(from_west, from_east, pair_a, pair_b):
    upper = (iota(0) // RIM) != odd_row()
    for d in range(from_west.shape[0]):
        p, q = from_west[d], row_roll(from_east[d], RIM)
        pair_a[d] = jnp.where(upper, p, q)
        pair_b[d] = jnp.where(upper, q, p)


def unpair(a, b):
    from_a = (iota(0) // RIM) == odd_row()
    return jnp.where(from_a, a, b), row_roll(jnp.where(from_a, b, a), RIM)


def coefficients(wet, wet_up, wet_down, u, v):
    sub = iota(0)
    first, last = sub == 0, sub == ROWS - 1
    north_wet = north(*wet, last)
    out = []
    for h in range(2):
        east_open = wet[h] * east(wet[h])
        north_open = wet[h] * north_wet[h]
        hu, hv = 0.5 * u[h], 0.5 * v[h]
        c = dict(
            east_open=east_open,
            north_open=north_open,
            p=east_open * (hu + HORIZ),
            q=east_open * (HORIZ - hu),
            r=north_open * (hv + HORIZ),
            s=north_open * (HORIZ - hv),
            up=None if wet_up is None else (VERT * wet[h]) * wet_up[h],
            down=None if wet_down is None else (VERT * wet[h]) * wet_down[h],
        )
        c["pw"], c["qw"] = west(c["p"]), west(c["q"])
        out.append(c)
    rs, ss = south(out[0]["r"], out[1]["r"], first), south(out[0]["s"], out[1]["s"], first)
    for h in range(2):
        c = out[h]
        c["rs"], c["ss"] = rs[h], ss[h]
        centre = wet[h] - ((c["p"] + c["qw"]) + (c["r"] + c["ss"]))
        for side in ("up", "down"):
            if c[side] is not None:
                centre = centre - c[side]
        c["centre"] = centre
    return out


FORWARD = ("q", "pw", "s", "rs")
BACKWARD = ("p", "qw", "r", "ss")


def combine(coef, names, x, e, w, n, s, up, down):
    out = (coef("centre") * x + coef(names[0]) * e) + (coef(names[1]) * w + coef(names[2]) * n)
    out = out + coef(names[3]) * s
    if up is not None:
        out = out + coef("up") * up
    if down is not None:
        out = out + coef("down") * down
    return out


COEFS = ("centre", "p", "q", "pw", "qw", "r", "s", "rs", "ss", "up", "down", "east_open", "north_open")


def main_kernel(trac, cot, east_vel, north_vel, mask, count, pair_a, pair_b, adj_t, adj_e, adj_n, edge_rim, state, sums, coef):
    n_trac, lev = trac.shape[:2]
    sub = iota(0)
    first, last = sub == 0, sub == ROWS - 1

    rims = {}
    for t in range(n_trac):
        for k in range(lev):
            c, b = unpair(pair_a[t * lev + k], pair_b[t * lev + k])
            state[0, t, k, 0] = trac[t, k]
            state[0, t, k, 1] = c
            state[2, t, k, 0] = cot[t, k]
            state[2, t, k, 1] = b
            rims[t, k], rims[n_trac + t, k] = c, b
    wet_at = (n_trac + 1) * lev
    count_own = wet_count(mask[...], count[...])
    count_rim = inside_rows(unpair(pair_a[wet_at], pair_b[wet_at])[0])
    wet = [tuple(jnp.where(x > k, 1.0, 0.0) for x in (count_own, count_rim)) for k in range(lev)]
    for k in range(lev):
        u_rim, v_rim = unpair(pair_a[n_trac * lev + k], pair_b[n_trac * lev + k])
        rims[2 * n_trac, k], rims[2 * n_trac + 1, k] = u_rim, v_rim
        rims[2 * n_trac + 2, k] = count_rim
        made = coefficients(
            wet[k],
            wet[k + 1] if k + 1 < lev else None,
            wet[k - 1] if k else None,
            (east_vel[k], u_rim),
            (north_vel[k], v_rim),
        )
        for h in range(2):
            for i, name in enumerate(COEFS):
                if made[h][name] is not None:
                    coef[i, k, h] = made[h][name]
    for f in range(2 * n_trac + 3):
        edge_rim[f] = edge_of([rims[f, k] for k in range(lev)])

    def neighbours(buf, t, k):
        own, rim = state[buf, t, k, 0], state[buf, t, k, 1]
        n, s = north(own, rim, last), south(own, rim, first)
        return (own, rim), (east(own), east(rim)), (west(own), west(rim)), n, s

    def apply(buf, t, k, near, names, halves):
        x, e, w, n, s = near
        for h in halves:
            up = state[buf, t, k + 1, h] if k + 1 < lev else None
            down = state[buf, t, k - 1, h] if k else None
            get = lambda name: coef[COEFS.index(name), k, h]
            yield h, combine(get, names, x[h], e[h], w[h], n[h], s[h], up, down)

    for step in range(STEPS):
        src, dst = step % 2, (step + 1) % 2
        for k in range(lev):
            for t in range(n_trac):
                if step < STEPS - 1:
                    near = neighbours(src, t, k)
                    for h, new in apply(src, t, k, near, FORWARD, (0, 1)):
                        state[dst, t, k, h] = new
                    x, e, n = near[0][0], near[1][0], near[3][0]
                else:
                    x, rim = state[src, t, k, 0], state[src, t, k, 1]
                    e, n = east(x), north(x, rim, last)[0]
                sums[step, 0, t, k] = x + e
                sums[step, 1, t, k] = x + n
    for step in reversed(range(STEPS)):
        src, dst = 2 + (STEPS - 1 - step) % 2, 2 + (STEPS - step) % 2
        for k in range(lev):
            acc_e = acc_n = None
            for t in range(n_trac):
                near = neighbours(src, t, k)
                for h, new in apply(src, t, k, near, BACKWARD, (0, 1) if step else (0,)):
                    if step:
                        state[dst, t, k, h] = new
                    else:
                        adj_t[t, k] = new
                x, e, n = near[0][0], near[1][0], near[3][0]
                term_e = sums[step, 0, t, k] * (e - x)
                term_n = sums[step, 1, t, k] * (n - x)
                acc_e = term_e if acc_e is None else acc_e + term_e
                acc_n = term_n if acc_n is None else acc_n + term_n
            if step < STEPS - 1:
                acc_e, acc_n = acc_e + adj_e[k], acc_n + adj_n[k]
            if step == 0:
                acc_e = acc_e * (0.5 * coef[COEFS.index("east_open"), k, 0])
                acc_n = acc_n * (0.5 * coef[COEFS.index("north_open"), k, 0])
            adj_e[k] = acc_e
            adj_n[k] = acc_n


def edge_kernel(edge, edge_rim, from_west, from_east, pair_a, pair_b, main_t, main_e, main_n, adj_t, adj_e, adj_n):
    n_trac, lev = main_t.shape[:2]
    n_fields = edge.shape[0]
    sub, lane = iota(0), iota(1)
    first, last = sub == 0, sub == ROWS - 1
    quarter = (lane % SLOT) // RIM
    corners = [unpair(pair_a[d], pair_b[d]) for d in range(from_west.shape[0])]

    def field(f, side):
        d, g = divmod(f, SLOT // RIM)
        shift = 0 if f == n_fields - 1 and g == 0 else 8 - RIM * g
        sent = (from_west, from_east)[side]
        own = jnp.where(quarter == 1 + side, lane_roll(sent[d], shift), edge[f])
        rim = jnp.where(quarter == 1 + side, lane_roll(corners[d][side], shift), edge_rim[f])
        return own, rim

    level = lane // SLOT
    out_e, out_n, out_t = [], [], []
    for side in range(2):
        own, rim = field(n_fields - 1, side)
        levels = level.astype(F32)
        wet = tuple(jnp.where(x > levels, 1.0, 0.0) for x in (own, inside_rows(rim)))
        up = tuple(jnp.where(level < lev - 1, lane_roll(x, -SLOT), 0.0) for x in wet)
        down = tuple(jnp.where(level > 0, lane_roll(x, SLOT), 0.0) for x in wet)
        made = coefficients(wet, up, down, field(2 * n_trac, side), field(2 * n_trac + 1, side))

        def near(x):
            n, s = north(*x, last), south(*x, first)
            return x, tuple(map(east, x)), tuple(map(west, x)), n, s

        def apply(about, names, halves):
            x, e, w, n, s = about
            out = []
            for h in halves:
                up, down = lane_roll(x[h], -SLOT), lane_roll(x[h], SLOT)
                out.append(combine(made[h].__getitem__, names, x[h], e[h], w[h], n[h], s[h], up, down))
            return tuple(out)

        state = [field(t, side) for t in range(n_trac)]
        lam = [field(n_trac + t, side) for t in range(n_trac)]
        sums = []
        for step in range(STEPS):
            about = [near(x) for x in state]
            sums.append([(a[0][0] + a[1][0], a[0][0] + a[3][0]) for a in about])
            if step < STEPS - 1:
                state = [apply(a, FORWARD, (0, 1)) for a in about]
        acc_e = acc_n = None
        for step in reversed(range(STEPS)):
            about = [near(x) for x in lam]
            for t, a in enumerate(about):
                x, e, n = a[0][0], a[1][0], a[3][0]
                term_e, term_n = sums[step][t][0] * (e - x), sums[step][t][1] * (n - x)
                acc_e = term_e if acc_e is None else acc_e + term_e
                acc_n = term_n if acc_n is None else acc_n + term_n
            lam = [apply(a, BACKWARD, (0, 1) if step else (0,)) for a in about]
        out_t.append([x[0] for x in lam])
        out_e.append(acc_e * (0.5 * made[0]["east_open"]))
        out_n.append(acc_n * (0.5 * made[0]["north_open"]))

    at_west = quarter >= 2
    margin = (lane < RIM) | (lane >= LANES - RIM)

    def put(ref, index, k, both, main):
        ref[index] = jnp.where(margin, lane_roll(both, -(SLOT * k + SLOT // 2)), main[index])

    for t in range(n_trac):
        both = jnp.where(at_west, out_t[0][t], out_t[1][t])
        for k in range(lev):
            put(adj_t, (t, k), k, both, main_t)
    for ref, out, main in ((adj_e, out_e, main_e), (adj_n, out_n, main_n)):
        both = jnp.where(at_west, *out)
        for k in range(lev):
            put(ref, (k,), k, both, main)


def call(body, outs, args, scratch=(), space=pltpu.VMEM):
    shapes = [s if hasattr(s, "dtype") else jax.ShapeDtypeStruct(s, F32) for s in outs]
    return pl.pallas_call(
        body,
        out_shape=shapes,
        in_specs=[pl.BlockSpec(memory_space=space)] * len(args),
        out_specs=[pl.BlockSpec(memory_space=pltpu.VMEM)] * len(outs),
        scratch_shapes=[pltpu.VMEM(s, F32) if isinstance(s, tuple) else s for s in scratch],
        name=body.__name__,
        compiler_params=pltpu.CompilerParams(vmem_limit_bytes=VMEM),
    )(*args)


def on_device(tracers, cotangent, east_vel, north_vel, sea_mask, level_count):
    n_trac, lev, rows, cols = tracers.shape
    assert (rows, cols, lev * SLOT) == (ROWS, LANES, LANES)
    n_lon, n_lat = lax.axis_size("lon"), lax.axis_size("lat")
    assert n_lat % 2 == 0
    n_pairs = (n_trac + 1) * lev + 1
    n_fields = 2 * n_trac + 3
    n_sent = -(-n_fields * RIM // SLOT)
    tile = (rows, cols)

    def swap_a(x):
        with jax.named_scope("swap_a"):
            return lax.ppermute(x, "lat", [(j, j ^ 1) for j in range(n_lat)])

    def swap_b(x):
        with jax.named_scope("swap_b"):
            return lax.ppermute(x, "lat", [(j, (((j + 1) ^ 1) - 1) % n_lat) for j in range(n_lat)])

    def shift(x, by):
        with jax.named_scope("east" if by > 0 else "west"):
            return lax.ppermute(x, "lon", [(i, (i + by) % n_lon) for i in range(n_lon)])

    args = (tracers, cotangent, east_vel, north_vel, sea_mask, level_count)
    args = [pltpu.with_memory_space_constraint(a, pltpu.HBM) for a in args]
    *args, pair_a, pair_b, to_west, to_east, edge = call(
        pack_kernel,
        [jax.ShapeDtypeStruct(a.shape, a.dtype) for a in args]
        + [(n_pairs,) + tile] * 2
        + [(n_sent,) + tile] * 2
        + [(n_fields,) + tile],
        args,
        [pltpu.SemaphoreType.DMA((len(args),))],
        pltpu.HBM,
    )
    from_west = shift(to_east, 1)
    from_east = shift(to_west, -1)
    pair_b = swap_b(pair_b)
    pair_a = swap_a(pair_a)
    corner_a, corner_b = call(corner_kernel, [(n_sent,) + tile] * 2, (from_west, from_east))
    corner_a = swap_a(corner_a)
    corner_b = swap_b(corner_b)
    outs = [tracers.shape, east_vel.shape, north_vel.shape]
    *main, edge_rim = call(
        main_kernel,
        outs + [(n_fields,) + tile],
        (*args, pair_a, pair_b),
        [(4, n_trac, lev, 2) + tile, (STEPS, 2, n_trac, lev) + tile, (len(COEFS), lev, 2) + tile],
    )
    return tuple(
        call(edge_kernel, outs, (edge, edge_rim, from_west, from_east, corner_a, corner_b, *main))
    )


def solution(mesh):
    state, flat, cell = P(None, None, "lat", "lon"), P(None, "lat", "lon"), P("lat", "lon")
    return jax.shard_map(
        on_device,
        mesh=mesh,
        in_specs=(state, state, flat, flat, cell, cell),
        out_specs=(state, flat, flat),
        check_vma=False,
    )
```

```python
import jax
import jax.numpy as jnp
from jax import lax
from jax.experimental import pallas as pl
from jax.experimental.pallas import tpu as pltpu
from jax.sharding import PartitionSpec as P


STEPS = 4
HORIZ = 0.22
VERT = 0.05

ROWS = 8
LANES = 128
RIM = 4
SLOT = 16
F32 = jnp.float32
VMEM = 8 << 20


def iota(axis):
    return lax.broadcasted_iota(jnp.int32, (ROWS, LANES), axis)


def lane_roll(x, shift):
    shift %= LANES
    return x if shift == 0 else pltpu.roll(x, shift, 1)


def row_roll(x, shift):
    return pltpu.roll(x, shift % ROWS, 0)


def east(x):
    return lane_roll(x, -1)


def west(x):
    return lane_roll(x, 1)


def north(own, rim, last):
    a, b = row_roll(own, -1), row_roll(rim, -1)
    return jnp.where(last, b, a), jnp.where(last, a, b)


def south(own, rim, first):
    a, b = row_roll(own, 1), row_roll(rim, 1)
    return jnp.where(first, b, a), jnp.where(first, a, b)


def odd_row():
    return lax.rem(lax.axis_index("lat"), 2)


def wet_count(mask, count):
    return jnp.where(mask == 1, count, 0).astype(F32)


def edge_of(planes):
    slot = iota(1) // SLOT
    out = None
    for k, plane in enumerate(planes):
        moved = lane_roll(plane, SLOT * k + SLOT // 2)
        out = moved if out is None else jnp.where(slot == k, moved, out)
    return out


def inside_rows(rim):
    place, total = lax.axis_index("lat"), lax.axis_size("lat")
    sub = iota(0)
    keep = ((sub >= RIM) | (place < total - 1)) & ((sub < RIM) | (place > 0))
    return jnp.where(keep, rim, 0.0)


def pack_kernel(*refs):
    args, here, (pair_a, pair_b, to_west, to_east, edge, sems) = refs[:6], refs[6:12], refs[12:]
    copies = [pltpu.make_async_copy(a, b, sems.at[i]) for i, (a, b) in enumerate(zip(args, here))]
    for copy in copies:
        copy.start()
    for copy in copies:
        copy.wait()
    trac, cot, east_vel, north_vel, mask, count = here
    n_trac, lev = trac.shape[:2]
    upper = (iota(0) // RIM) != odd_row()

    def pair(index, p, q):
        q = row_roll(q, RIM)
        pair_a[index] = jnp.where(upper, p, q)
        pair_b[index] = jnp.where(upper, q, p)

    for t in range(n_trac):
        for k in range(lev):
            pair(t * lev + k, trac[t, k], cot[t, k])
    for k in range(lev):
        pair(n_trac * lev + k, east_vel[k], north_vel[k])
    wet = wet_count(mask[...], count[...])
    pair_a[(n_trac + 1) * lev] = wet
    pair_b[(n_trac + 1) * lev] = wet

    fields = [[trac[t, k] for k in range(lev)] for t in range(n_trac)]
    fields += [[cot[t, k] for k in range(lev)] for t in range(n_trac)]
    fields += [[ref[k] for k in range(lev)] for ref in (east_vel, north_vel)]
    fields += [[wet] * lev]
    quarter = (iota(1) % SLOT) // RIM
    west_out, east_out = {}, {}
    for f, planes in enumerate(fields):
        e = edge_of(planes)
        edge[f] = e
        d, g = divmod(f, SLOT // RIM)
        if f == len(fields) - 1 and g == 0:
            west_out[d] = east_out[d] = e
            continue
        moved = lane_roll(e, RIM * g - 8)
        if g == 0:
            west_out[d] = east_out[d] = moved
        else:
            west_out[d] = jnp.where(quarter == g, moved, west_out[d])
            east_out[d] = jnp.where(quarter == g - 1, moved, east_out[d])
    for d in west_out:
        to_west[d] = west_out[d]
        to_east[d] = east_out[d]


def corner_kernel(from_west, from_east, pair_a, pair_b):
    upper = (iota(0) // RIM) != odd_row()
    for d in range(from_west.shape[0]):
        p, q = from_west[d], row_roll(from_east[d], RIM)
        pair_a[d] = jnp.where(upper, p, q)
        pair_b[d] = jnp.where(upper, q, p)


def unpair(a, b):
    from_a = (iota(0) // RIM) == odd_row()
    return jnp.where(from_a, a, b), row_roll(jnp.where(from_a, b, a), RIM)


def coefficients(wet, wet_up, wet_down, u, v):
    sub = iota(0)
    first, last = sub == 0, sub == ROWS - 1
    north_wet = north(*wet, last)
    out = []
    for h in range(2):
        east_open = wet[h] * east(wet[h])
        north_open = wet[h] * north_wet[h]
        hu, hv = 0.5 * u[h], 0.5 * v[h]
        c = dict(
            east_open=east_open,
            north_open=north_open,
            p=east_open * (hu + HORIZ),
            q=east_open * (HORIZ - hu),
            r=north_open * (hv + HORIZ),
            s=north_open * (HORIZ - hv),
            up=None if wet_up is None else (VERT * wet[h]) * wet_up[h],
            down=None if wet_down is None else (VERT * wet[h]) * wet_down[h],
        )
        c["pw"], c["qw"] = west(c["p"]), west(c["q"])
        out.append(c)
    rs, ss = south(out[0]["r"], out[1]["r"], first), south(out[0]["s"], out[1]["s"], first)
    for h in range(2):
        c = out[h]
        c["rs"], c["ss"] = rs[h], ss[h]
        centre = wet[h] - ((c["p"] + c["qw"]) + (c["r"] + c["ss"]))
        for side in ("up", "down"):
            if c[side] is not None:
                centre = centre - c[side]
        c["centre"] = centre
    return out


FORWARD = ("q", "pw", "s", "rs")
BACKWARD = ("p", "qw", "r", "ss")


def combine(coef, names, x, e, w, n, s, up, down):
    out = (coef("centre") * x + coef(names[0]) * e) + (coef(names[1]) * w + coef(names[2]) * n)
    out = out + coef(names[3]) * s
    if up is not None:
        out = out + coef("up") * up
    if down is not None:
        out = out + coef("down") * down
    return out


COEFS = ("centre", "p", "q", "pw", "qw", "r", "s", "rs", "ss", "up", "down", "east_open", "north_open")


def main_kernel(trac, cot, east_vel, north_vel, mask, count, pair_a, pair_b, adj_t, adj_e, adj_n, edge_rim, state, sums, coef):
    n_trac, lev = trac.shape[:2]
    sub = iota(0)
    first, last = sub == 0, sub == ROWS - 1

    rims = {}
    for t in range(n_trac):
        for k in range(lev):
            c, b = unpair(pair_a[t * lev + k], pair_b[t * lev + k])
            state[0, t, k, 0] = trac[t, k]
            state[0, t, k, 1] = c
            state[2, t, k, 0] = cot[t, k]
            state[2, t, k, 1] = b
            rims[t, k], rims[n_trac + t, k] = c, b
    wet_at = (n_trac + 1) * lev
    count_own = wet_count(mask[...], count[...])
    count_rim = inside_rows(unpair(pair_a[wet_at], pair_b[wet_at])[0])
    wet = [tuple(jnp.where(x > k, 1.0, 0.0) for x in (count_own, count_rim)) for k in range(lev)]
    for k in range(lev):
        u_rim, v_rim = unpair(pair_a[n_trac * lev + k], pair_b[n_trac * lev + k])
        rims[2 * n_trac, k], rims[2 * n_trac + 1, k] = u_rim, v_rim
        rims[2 * n_trac + 2, k] = count_rim
        made = coefficients(
            wet[k],
            wet[k + 1] if k + 1 < lev else None,
            wet[k - 1] if k else None,
            (east_vel[k], u_rim),
            (north_vel[k], v_rim),
        )
        for h in range(2):
            for i, name in enumerate(COEFS):
                if made[h][name] is not None:
                    coef[i, k, h] = made[h][name]
    for f in range(2 * n_trac + 3):
        edge_rim[f] = edge_of([rims[f, k] for k in range(lev)])

    def neighbours(buf, t, k):
        own, rim = state[buf, t, k, 0], state[buf, t, k, 1]
        n, s = north(own, rim, last), south(own, rim, first)
        return (own, rim), (east(own), east(rim)), (west(own), west(rim)), n, s

    def apply(buf, t, k, near, names, halves):
        x, e, w, n, s = near
        for h in halves:
            up = state[buf, t, k + 1, h] if k + 1 < lev else None
            down = state[buf, t, k - 1, h] if k else None
            get = lambda name: coef[COEFS.index(name), k, h]
            yield h, combine(get, names, x[h], e[h], w[h], n[h], s[h], up, down)

    for step in range(STEPS):
        src, dst = step % 2, (step + 1) % 2
        for k in range(lev):
            for t in range(n_trac):
                if step < STEPS - 1:
                    near = neighbours(src, t, k)
                    for h, new in apply(src, t, k, near, FORWARD, (0, 1)):
                        state[dst, t, k, h] = new
                    x, e, n = near[0][0], near[1][0], near[3][0]
                else:
                    x, rim = state[src, t, k, 0], state[src, t, k, 1]
                    e, n = east(x), north(x, rim, last)[0]
                sums[step, 0, t, k] = x + e
                sums[step, 1, t, k] = x + n
    for step in reversed(range(STEPS)):
        src, dst = 2 + (STEPS - 1 - step) % 2, 2 + (STEPS - step) % 2
        for k in range(lev):
            acc_e = acc_n = None
            for t in range(n_trac):
                near = neighbours(src, t, k)
                for h, new in apply(src, t, k, near, BACKWARD, (0, 1) if step else (0,)):
                    if step:
                        state[dst, t, k, h] = new
                    else:
                        adj_t[t, k] = new
                x, e, n = near[0][0], near[1][0], near[3][0]
                term_e = sums[step, 0, t, k] * (e - x)
                term_n = sums[step, 1, t, k] * (n - x)
                acc_e = term_e if acc_e is None else acc_e + term_e
                acc_n = term_n if acc_n is None else acc_n + term_n
            if step < STEPS - 1:
                acc_e, acc_n = acc_e + adj_e[k], acc_n + adj_n[k]
            if step == 0:
                acc_e = acc_e * (0.5 * coef[COEFS.index("east_open"), k, 0])
                acc_n = acc_n * (0.5 * coef[COEFS.index("north_open"), k, 0])
            adj_e[k] = acc_e
            adj_n[k] = acc_n


def edge_kernel(edge, edge_rim, from_west, from_east, pair_a, pair_b, main_t, main_e, main_n, adj_t, adj_e, adj_n):
    n_trac, lev = main_t.shape[:2]
    n_fields = edge.shape[0]
    sub, lane = iota(0), iota(1)
    first, last = sub == 0, sub == ROWS - 1
    quarter = (lane % SLOT) // RIM
    corners = [unpair(pair_a[d], pair_b[d]) for d in range(from_west.shape[0])]

    def field(f, side):
        d, g = divmod(f, SLOT // RIM)
        shift = 0 if f == n_fields - 1 and g == 0 else 8 - RIM * g
        sent = (from_west, from_east)[side]
        own = jnp.where(quarter == 1 + side, lane_roll(sent[d], shift), edge[f])
        rim = jnp.where(quarter == 1 + side, lane_roll(corners[d][side], shift), edge_rim[f])
        return own, rim

    level = lane // SLOT
    out_e, out_n, out_t = [], [], []
    for side in range(2):
        own, rim = field(n_fields - 1, side)
        levels = level.astype(F32)
        wet = tuple(jnp.where(x > levels, 1.0, 0.0) for x in (own, inside_rows(rim)))
        up = tuple(jnp.where(level < lev - 1, lane_roll(x, -SLOT), 0.0) for x in wet)
        down = tuple(jnp.where(level > 0, lane_roll(x, SLOT), 0.0) for x in wet)
        made = coefficients(wet, up, down, field(2 * n_trac, side), field(2 * n_trac + 1, side))

        def near(x):
            n, s = north(*x, last), south(*x, first)
            return x, tuple(map(east, x)), tuple(map(west, x)), n, s

        def apply(about, names, halves):
            x, e, w, n, s = about
            out = []
            for h in halves:
                up, down = lane_roll(x[h], -SLOT), lane_roll(x[h], SLOT)
                out.append(combine(made[h].__getitem__, names, x[h], e[h], w[h], n[h], s[h], up, down))
            return tuple(out)

        state = [field(t, side) for t in range(n_trac)]
        lam = [field(n_trac + t, side) for t in range(n_trac)]
        sums = []
        for step in range(STEPS):
            about = [near(x) for x in state]
            sums.append([(a[0][0] + a[1][0], a[0][0] + a[3][0]) for a in about])
            if step < STEPS - 1:
                state = [apply(a, FORWARD, (0, 1)) for a in about]
        acc_e = acc_n = None
        for step in reversed(range(STEPS)):
            about = [near(x) for x in lam]
            for t, a in enumerate(about):
                x, e, n = a[0][0], a[1][0], a[3][0]
                term_e, term_n = sums[step][t][0] * (e - x), sums[step][t][1] * (n - x)
                acc_e = term_e if acc_e is None else acc_e + term_e
                acc_n = term_n if acc_n is None else acc_n + term_n
            lam = [apply(a, BACKWARD, (0, 1) if step else (0,)) for a in about]
        out_t.append([x[0] for x in lam])
        out_e.append(acc_e * (0.5 * made[0]["east_open"]))
        out_n.append(acc_n * (0.5 * made[0]["north_open"]))

    at_west = quarter >= 2
    margin = (lane < RIM) | (lane >= LANES - RIM)

    def put(ref, index, k, both, main):
        ref[index] = jnp.where(margin, lane_roll(both, -(SLOT * k + SLOT // 2)), main[index])

    for t in range(n_trac):
        both = jnp.where(at_west, out_t[0][t], out_t[1][t])
        for k in range(lev):
            put(adj_t, (t, k), k, both, main_t)
    for ref, out, main in ((adj_e, out_e, main_e), (adj_n, out_n, main_n)):
        both = jnp.where(at_west, *out)
        for k in range(lev):
            put(ref, (k,), k, both, main)


def call(body, outs, args, scratch=(), space=pltpu.VMEM):
    shapes = [s if hasattr(s, "dtype") else jax.ShapeDtypeStruct(s, F32) for s in outs]
    return pl.pallas_call(
        body,
        out_shape=shapes,
        in_specs=[pl.BlockSpec(memory_space=space)] * len(args),
        out_specs=[pl.BlockSpec(memory_space=pltpu.VMEM)] * len(outs),
        scratch_shapes=[pltpu.VMEM(s, F32) if isinstance(s, tuple) else s for s in scratch],
        compiler_params=pltpu.CompilerParams(vmem_limit_bytes=VMEM),
    )(*args)


def adjoint(tracers, cotangent, east_vel, north_vel, sea_mask, level_count):
    n_trac, lev, rows, cols = tracers.shape
    assert (rows, cols, lev * SLOT) == (ROWS, LANES, LANES)
    n_lon, n_lat = lax.axis_size("lon"), lax.axis_size("lat")
    assert n_lat % 2 == 0
    n_pairs = (n_trac + 1) * lev + 1
    n_fields = 2 * n_trac + 3
    n_sent = -(-n_fields * RIM // SLOT)
    tile = (rows, cols)

    def swap_a(x):
        return lax.ppermute(x, "lat", [(j, j ^ 1) for j in range(n_lat)])

    def swap_b(x):
        pairs = []
        for i in range(n_lon):
            for j in range(n_lat):
                end = j in (0, n_lat - 1)
                to = (i ^ 1, j) if end else (i, ((j + 1) ^ 1) - 1)
                pairs.append((i * n_lat + j, to[0] * n_lat + to[1]))
        return lax.ppermute(x, ("lon", "lat"), pairs)

    def shift(x, by):
        return lax.ppermute(x, "lon", [(i, (i + by) % n_lon) for i in range(n_lon)])

    args = (tracers, cotangent, east_vel, north_vel, sea_mask, level_count)
    args = [pltpu.with_memory_space_constraint(a, pltpu.HBM) for a in args]
    *args, pair_a, pair_b, to_west, to_east, edge = call(
        pack_kernel,
        [jax.ShapeDtypeStruct(a.shape, a.dtype) for a in args]
        + [(n_pairs,) + tile] * 2
        + [(n_sent,) + tile] * 2
        + [(n_fields,) + tile],
        args,
        [pltpu.SemaphoreType.DMA((len(args),))],
        pltpu.HBM,
    )
    from_west = shift(to_east, 1)
    from_east = shift(to_west, -1)
    pair_b = swap_b(pair_b)
    pair_a = swap_a(pair_a)
    corner_a, corner_b = call(corner_kernel, [(n_sent,) + tile] * 2, (from_west, from_east))
    corner_a = swap_a(corner_a)
    corner_b = swap_b(corner_b)
    outs = [tracers.shape, east_vel.shape, north_vel.shape]
    *main, edge_rim = call(
        main_kernel,
        outs + [(n_fields,) + tile],
        (*args, pair_a, pair_b),
        [(4, n_trac, lev, 2) + tile, (STEPS, 2, n_trac, lev) + tile, (len(COEFS), lev, 2) + tile],
    )
    return tuple(
        call(edge_kernel, outs, (edge, edge_rim, from_west, from_east, corner_a, corner_b, *main))
    )


def solution(mesh):
    state, flat, cell = P(None, None, "lat", "lon"), P(None, "lat", "lon"), P("lat", "lon")
    return jax.shard_map(
        adjoint,
        mesh=mesh,
        in_specs=(state, state, flat, flat, cell, cell),
        out_specs=(state, flat, flat),
        check_vma=False,
    )
```

```python
import jax
import jax.numpy as jnp
from jax import lax
from jax.experimental import pallas as pl
from jax.experimental.pallas import tpu as pltpu
from jax.sharding import PartitionSpec as P


STEPS = 4
HORIZ = 0.22
VERT = 0.05

ROWS = 8
LANES = 128
RIM = 4
SLOT = 16
F32 = jnp.float32
VMEM = 8 << 20


def iota(axis):
    return lax.broadcasted_iota(jnp.int32, (ROWS, LANES), axis)


def lane_roll(x, shift):
    shift %= LANES
    return x if shift == 0 else pltpu.roll(x, shift, 1)


def row_roll(x, shift):
    return pltpu.roll(x, shift % ROWS, 0)


def east(x):
    return lane_roll(x, -1)


def west(x):
    return lane_roll(x, 1)


def north(own, rim, last):
    a, b = row_roll(own, -1), row_roll(rim, -1)
    return jnp.where(last, b, a), jnp.where(last, a, b)


def south(own, rim, first):
    a, b = row_roll(own, 1), row_roll(rim, 1)
    return jnp.where(first, b, a), jnp.where(first, a, b)


def odd_row():
    return lax.rem(lax.axis_index("lat"), 2)


def wet_count(mask, count):
    return jnp.where(mask == 1, count, 0).astype(F32)


def edge_of(planes):
    slot = iota(1) // SLOT
    out = None
    for k, plane in enumerate(planes):
        moved = lane_roll(plane, SLOT * k + SLOT // 2)
        out = moved if out is None else jnp.where(slot == k, moved, out)
    return out


def inside_rows(rim):
    place, total = lax.axis_index("lat"), lax.axis_size("lat")
    sub = iota(0)
    keep = ((sub >= RIM) | (place < total - 1)) & ((sub < RIM) | (place > 0))
    return jnp.where(keep, rim, 0.0)


def pack_kernel(*refs):
    args, here, (pair_a, pair_b, to_west, to_east, edge, sems) = refs[:6], refs[6:12], refs[12:]
    copies = [pltpu.make_async_copy(a, b, sems.at[i]) for i, (a, b) in enumerate(zip(args, here))]
    for copy in copies:
        copy.start()
    for copy in copies:
        copy.wait()
    trac, cot, east_vel, north_vel, mask, count = here
    n_trac, lev = trac.shape[:2]
    upper = (iota(0) // RIM) != odd_row()

    def pair(index, p, q):
        q = row_roll(q, RIM)
        pair_a[index] = jnp.where(upper, p, q)
        pair_b[index] = jnp.where(upper, q, p)

    for t in range(n_trac):
        for k in range(lev):
            pair(t * lev + k, trac[t, k], cot[t, k])
    for k in range(lev):
        pair(n_trac * lev + k, east_vel[k], north_vel[k])
    wet = wet_count(mask[...], count[...])
    pair_a[(n_trac + 1) * lev] = wet
    pair_b[(n_trac + 1) * lev] = wet

    fields = [[trac[t, k] for k in range(lev)] for t in range(n_trac)]
    fields += [[cot[t, k] for k in range(lev)] for t in range(n_trac)]
    fields += [[ref[k] for k in range(lev)] for ref in (east_vel, north_vel)]
    fields += [[wet] * lev]
    quarter = (iota(1) % SLOT) // RIM
    west_out, east_out = {}, {}
    for f, planes in enumerate(fields):
        e = edge_of(planes)
        edge[f] = e
        d, g = divmod(f, SLOT // RIM)
        if f == len(fields) - 1 and g == 0:
            west_out[d] = east_out[d] = e
            continue
        moved = lane_roll(e, RIM * g - 8)
        if g == 0:
            west_out[d] = east_out[d] = moved
        else:
            west_out[d] = jnp.where(quarter == g, moved, west_out[d])
            east_out[d] = jnp.where(quarter == g - 1, moved, east_out[d])
    for d in west_out:
        to_west[d] = west_out[d]
        to_east[d] = east_out[d]


def corner_kernel(from_west, from_east, pair_a, pair_b):
    upper = (iota(0) // RIM) != odd_row()
    for d in range(from_west.shape[0]):
        p, q = from_west[d], row_roll(from_east[d], RIM)
        pair_a[d] = jnp.where(upper, p, q)
        pair_b[d] = jnp.where(upper, q, p)


def unpair(a, b):
    from_a = (iota(0) // RIM) == odd_row()
    return jnp.where(from_a, a, b), row_roll(jnp.where(from_a, b, a), RIM)


def velocity_terms(wet, east_wet, north_wet, u, v):
    east_open, north_open = wet * east_wet, wet * north_wet
    hu, hv = 0.5 * u, 0.5 * v
    p, q = east_open * (hu + HORIZ), east_open * (HORIZ - hu)
    r, s = north_open * (hv + HORIZ), north_open * (HORIZ - hv)
    return dict(east_open=east_open, north_open=north_open, p=p, q=q, r=r, s=s, pw=west(p), qw=west(q))


def finish(c, wet, rs, ss, wet_up, wet_down):
    c["rs"], c["ss"] = rs, ss
    centre = wet - ((c["p"] + c["qw"]) + (c["r"] + ss))
    for side, other in (("up", wet_up), ("down", wet_down)):
        if other is not None:
            c[side] = (VERT * wet) * other
            centre = centre - c[side]
    c["centre"] = centre
    return c


def coefficients(wet, wet_up, wet_down, u, v):
    sub = iota(0)
    first, last = sub == 0, sub == ROWS - 1
    north_wet = north(*wet, last)
    out = [velocity_terms(wet[h], east(wet[h]), north_wet[h], u[h], v[h]) for h in range(2)]
    rs, ss = (south(out[0][x], out[1][x], first) for x in "rs")
    for h in range(2):
        finish(out[h], wet[h], rs[h], ss[h], wet_up and wet_up[h], wet_down and wet_down[h])
    return out


FORWARD = ("q", "pw", "s", "rs")
BACKWARD = ("p", "qw", "r", "ss")
COEFS = ("centre", "p", "q", "pw", "qw", "r", "s", "rs", "ss", "up", "down", "east_open", "north_open")


def combine(coef, names, x, e, w, n, s, up, down):
    out = (coef("centre") * x + coef(names[0]) * e) + (coef(names[1]) * w + coef(names[2]) * n)
    out = out + coef(names[3]) * s
    if up is not None:
        out = out + coef("up") * up
    if down is not None:
        out = out + coef("down") * down
    return out


def add(total, term):
    return term if total is None else total + term


def packed_edges(pairs, n_trac, lev):
    groups = [[pairs[i * lev + k] for k in range(lev)] for i in range(n_trac + 1)]
    return [edge_of(g) for g in groups] + [edge_of([pairs[(n_trac + 1) * lev]] * lev)]


def near_kernel(trac, cot, east_vel, north_vel, mask, count, pair_a, adj_t, adj_e, adj_n, past, past_adj, edge_a, rims, sums, coef):
    n_trac, lev = trac.shape[:2]
    sub = iota(0)
    first, last = sub == 0, sub == ROWS - 1
    for i, e in enumerate(packed_edges(pair_a, n_trac, lev)):
        edge_a[i] = e

    def rim(index):
        x = pair_a[index]
        return x, row_roll(x, RIM)

    for t in range(n_trac):
        for k in range(lev):
            rims[0, t, k], rims[2, t, k] = rim(t * lev + k)
    own_side = (sub // RIM) == odd_row()
    count_own = wet_count(mask[...], count[...])
    count_rim = jnp.where(own_side, pair_a[(n_trac + 1) * lev], 0.0)
    wet = [tuple(jnp.where(x > k, 1.0, 0.0) for x in (count_own, count_rim)) for k in range(lev)]
    for k in range(lev):
        u_rim, v_rim = rim(n_trac * lev + k)
        made = coefficients(
            wet[k],
            wet[k + 1] if k + 1 < lev else None,
            wet[k - 1] if k else None,
            (east_vel[k], u_rim),
            (north_vel[k], v_rim),
        )
        for h in range(2):
            for name, value in made[h].items():
                coef[COEFS.index(name), k, h] = value

    def states(own, buf):
        return lambda t, k: (own[t, k], rims[buf, t, k])

    def neighbours(pair):
        own, out = pair
        n, s = north(own, out, last), south(own, out, first)
        return (own, out), (east(own), east(out)), (west(own), west(out)), n, s

    def apply(get, k, t, about, names, h):
        x, e, w, n, s = about
        up = get(t, k + 1)[h] if k + 1 < lev else None
        down = get(t, k - 1)[h] if k else None
        return combine(lambda name: coef[COEFS.index(name), k, h], names, x[h], e[h], w[h], n[h], s[h], up, down)

    for step in range(STEPS):
        get = states(past.at[step - 1] if step else trac, step % 2)
        for k in range(lev):
            for t in range(n_trac):
                if step < STEPS - 1:
                    about = neighbours(get(t, k))
                    past[step, t, k] = apply(get, k, t, about, FORWARD, 0)
                    rims[(step + 1) % 2, t, k] = apply(get, k, t, about, FORWARD, 1)
                    x, e, n = about[0][0], about[1][0], about[3][0]
                else:
                    x, out = get(t, k)
                    e, n = east(x), north(x, out, last)[0]
                sums[step, 0, t, k] = x + e
                sums[step, 1, t, k] = x + n
    for done, step in enumerate(reversed(range(STEPS))):
        get = states(past_adj.at[done - 1] if done else cot, 2 + done % 2)
        for k in range(lev):
            acc_e = acc_n = None
            for t in range(n_trac):
                about = neighbours(get(t, k))
                new = apply(get, k, t, about, BACKWARD, 0)
                if step:
                    past_adj[done, t, k] = new
                    rims[2 + (done + 1) % 2, t, k] = apply(get, k, t, about, BACKWARD, 1)
                else:
                    adj_t[t, k] = new
                x, e, n = about[0][0], about[1][0], about[3][0]
                acc_e = add(acc_e, sums[step, 0, t, k] * (e - x))
                acc_n = add(acc_n, sums[step, 1, t, k] * (n - x))
            if done:
                acc_e, acc_n = acc_e + adj_e[k], acc_n + adj_n[k]
            if step == 0:
                acc_e = acc_e * (0.5 * coef[COEFS.index("east_open"), k, 0])
                acc_n = acc_n * (0.5 * coef[COEFS.index("north_open"), k, 0])
            adj_e[k] = acc_e
            adj_n[k] = acc_n


class Far:
    def __init__(self, args, pair_b, past, past_adj, state, sums, coef, acc):
        self.trac, self.cot, east_vel, north_vel, mask, count = args
        self.past, self.past_adj, self.state, self.sums, self.coef, self.acc = past, past_adj, state, sums, coef, acc
        n_trac, lev = self.n_trac, self.lev = self.trac.shape[:2]
        sub = iota(0)
        self.first, self.last = sub == 0, sub == ROWS - 1
        self.rim = (sub // RIM) == odd_row()

        def both(index, p, q):
            x = pair_b[index]
            return self.join(row_roll(x, RIM), p), self.join(x, q)

        for t in range(n_trac):
            for k in range(lev):
                state[0, t, k], state[2, t, k] = both(t * lev + k, self.trac[t, k], self.cot[t, k])
        place = lax.axis_index("lat")
        outside = (place == 0) | (place == lax.axis_size("lat") - 1)
        count_own = wet_count(mask[...], count[...])
        count_rim = row_roll(pair_b[(n_trac + 1) * lev], RIM)
        count_far = self.join(jnp.where(outside, jnp.zeros_like(count_rim), count_rim), count_own)
        own = [jnp.where(count_own > k, 1.0, 0.0) for k in range(lev)]
        far = [jnp.where(count_far > k, 1.0, 0.0) for k in range(lev)]
        for k in range(lev):
            u, v = both(n_trac * lev + k, east_vel[k], north_vel[k])
            beyond = velocity_terms(own[k], own[k], row_roll(own[k], -1), north_vel[k], north_vel[k])
            made = velocity_terms(far[k], east(far[k]), self.north(far[k], own[k]), u, v)
            rs, ss = (self.south(made[x], beyond[x]) for x in "rs")
            finish(made, far[k], rs, ss, far[k + 1] if k + 1 < lev else None, far[k - 1] if k else None)
            for name, value in made.items():
                coef[COEFS.index(name), k] = value

    def join(self, rim, own):
        return jnp.where(self.rim, rim, row_roll(own, RIM))

    def north(self, x, beyond):
        return jnp.where(self.last, row_roll(beyond, 3), row_roll(x, -1))

    def south(self, x, beyond):
        return jnp.where(self.first, row_roll(beyond, -3), row_roll(x, 1))

    def apply(self, buf, t, k, about, names):
        up = self.state[buf, t, k + 1] if k + 1 < self.lev else None
        down = self.state[buf, t, k - 1] if k else None
        return combine(lambda name: self.coef[COEFS.index(name), k], names, *about, up, down)

    def forward(self, step):
        src, dst = step % 2, (step + 1) % 2
        own = self.past.at[step - 1] if step else self.trac
        for k in range(self.lev):
            for t in range(self.n_trac):
                x, beyond = self.state[src, t, k], own[t, k]
                e, n = east(x), self.north(x, beyond)
                self.sums[step, 0, t, k] = x + e
                self.sums[step, 1, t, k] = x + n
                if step < STEPS - 1:
                    about = x, e, west(x), n, self.south(x, beyond)
                    self.state[dst, t, k] = self.apply(src, t, k, about, FORWARD)

    def backward(self, done):
        step = STEPS - 1 - done
        src, dst = 2 + done % 2, 2 + (done + 1) % 2
        own = self.past_adj.at[done - 1] if done else self.cot
        for k in range(self.lev):
            acc_e = acc_n = None
            for t in range(self.n_trac):
                x, beyond = self.state[src, t, k], own[t, k]
                e, n = east(x), self.north(x, beyond)
                about = x, e, west(x), n, self.south(x, beyond)
                self.state[dst, t, k] = self.apply(src, t, k, about, BACKWARD)
                acc_e = add(acc_e, self.sums[step, 0, t, k] * (e - x))
                acc_n = add(acc_n, self.sums[step, 1, t, k] * (n - x))
            if done:
                acc_e, acc_n = acc_e + self.acc[0, k], acc_n + self.acc[1, k]
            self.acc[0, k], self.acc[1, k] = acc_e, acc_n

    def merged(self, t, k, near):
        return jnp.where(self.rim, row_roll(self.state[2 + STEPS % 2, t, k], RIM), near)

    def merged_gradient(self, i, k, near):
        opened = self.coef[COEFS.index(("east_open", "north_open")[i]), k]
        return jnp.where(self.rim, row_roll(self.acc[i, k] * (0.5 * opened), RIM), near)


class Strip:
    def __init__(self, side, n_trac, lev, edge, rims, sent, corners):
        self.n_trac = n_trac
        n_fields = edge.shape[0]
        sub, lane = iota(0), iota(1)
        self.first, self.last = sub == 0, sub == ROWS - 1
        level = lane // SLOT
        from_side = (lane % SLOT) // RIM == 1 + side

        def field(f):
            d, g = divmod(f, SLOT // RIM)
            shift = 0 if f == n_fields - 1 and g == 0 else 8 - RIM * g
            own = jnp.where(from_side, lane_roll(sent[d], shift), edge[f])
            rim = jnp.where(from_side, lane_roll(corners[d], shift), rims[f])
            return own, rim

        own, rim = field(n_fields - 1)
        levels = level.astype(F32)
        wet = tuple(jnp.where(x > levels, 1.0, 0.0) for x in (own, inside_rows(rim)))
        up = tuple(jnp.where(level < lev - 1, lane_roll(x, -SLOT), 0.0) for x in wet)
        down = tuple(jnp.where(level > 0, lane_roll(x, SLOT), 0.0) for x in wet)
        self.made = coefficients(wet, up, down, field(2 * n_trac), field(2 * n_trac + 1))
        self.state = [field(t) for t in range(n_trac)]
        self.lam = [field(n_trac + t) for t in range(n_trac)]
        self.sums, self.acc_e, self.acc_n = [], None, None

    def near(self, x):
        n, s = north(*x, self.last), south(*x, self.first)
        return x, tuple(map(east, x)), tuple(map(west, x)), n, s

    def apply(self, about, names, halves):
        x, e, w, n, s = about
        return tuple(
            combine(self.made[h].__getitem__, names, x[h], e[h], w[h], n[h], s[h], lane_roll(x[h], -SLOT), lane_roll(x[h], SLOT))
            for h in halves
        )

    def forward(self, step):
        about = [self.near(x) for x in self.state]
        self.sums.append([(a[0][0] + a[1][0], a[0][0] + a[3][0]) for a in about])
        if step < STEPS - 1:
            self.state = [self.apply(a, FORWARD, (0, 1)) for a in about]

    def backward(self, done):
        step = STEPS - 1 - done
        about = [self.near(x) for x in self.lam]
        for (sum_e, sum_n), a in zip(self.sums[step], about):
            x, e, n = a[0][0], a[1][0], a[3][0]
            self.acc_e = add(self.acc_e, sum_e * (e - x))
            self.acc_n = add(self.acc_n, sum_n * (n - x))
        self.lam = [self.apply(a, BACKWARD, (0, 1) if step else (0,)) for a in about]

    def gradients(self):
        own = self.made[0]
        return self.acc_e * (0.5 * own["east_open"]), self.acc_n * (0.5 * own["north_open"])


def far_kernel(*refs):
    args, refs = refs[:6], refs[6:]
    pair_b, near_t, near_e, near_n, past, past_adj, edge_a = refs[:7]
    adj_t, adj_e, adj_n, edge_rim, state, sums, coef, acc = refs[7:]
    n_trac, lev = near_t.shape[:2]

    for i, b in enumerate(packed_edges(pair_b, n_trac, lev)):
        p, q = unpair(edge_a[i], b)
        if i < n_trac:
            edge_rim[i], edge_rim[n_trac + i] = p, q
        elif i == n_trac:
            edge_rim[2 * n_trac], edge_rim[2 * n_trac + 1] = p, q
        else:
            edge_rim[2 * n_trac + 2] = p
    far = Far(args, pair_b, past, past_adj, state, sums, coef, acc)
    for step in range(STEPS):
        far.forward(step)
    for done in range(STEPS):
        far.backward(done)
    for k in range(lev):
        for t in range(n_trac):
            adj_t[t, k] = far.merged(t, k, near_t[t, k])
        adj_e[k] = far.merged_gradient(0, k, near_e[k])
        adj_n[k] = far.merged_gradient(1, k, near_n[k])


def edge_kernel(edge, edge_rim, from_west, from_east, corner_a, corner_b, main_t, main_e, main_n, adj_t, adj_e, adj_n):
    n_trac, lev = main_t.shape[:2]
    corners = [unpair(corner_a[d], corner_b[d]) for d in range(from_west.shape[0])]
    strips = [
        Strip(side, n_trac, lev, edge, edge_rim, sent, [c[side] for c in corners])
        for side, sent in enumerate((from_west, from_east))
    ]
    for step in range(STEPS):
        for part in strips:
            part.forward(step)
    for done in range(STEPS):
        for part in strips:
            part.backward(done)

    lane = iota(1)
    at_west = (lane % SLOT) // RIM >= 2
    margin = (lane < RIM) | (lane >= LANES - RIM)

    def put(ref, index, k, both, main):
        ref[index] = jnp.where(margin, lane_roll(both, -(SLOT * k + SLOT // 2)), main[index])

    for t in range(n_trac):
        both = jnp.where(at_west, strips[0].lam[t][0], strips[1].lam[t][0])
        for k in range(lev):
            put(adj_t, (t, k), k, both, main_t)
    for ref, main, *sides in zip((adj_e, adj_n), (main_e, main_n), *(s.gradients() for s in strips)):
        both = jnp.where(at_west, *sides)
        for k in range(lev):
            put(ref, (k,), k, both, main)


def call(body, outs, args, scratch=(), space=pltpu.VMEM):
    shapes = [s if hasattr(s, "dtype") else jax.ShapeDtypeStruct(s, F32) for s in outs]
    return pl.pallas_call(
        body,
        out_shape=shapes,
        in_specs=[pl.BlockSpec(memory_space=space)] * len(args),
        out_specs=[pl.BlockSpec(memory_space=pltpu.VMEM)] * len(outs),
        scratch_shapes=[pltpu.VMEM(s, F32) if isinstance(s, tuple) else s for s in scratch],
        compiler_params=pltpu.CompilerParams(vmem_limit_bytes=VMEM),
    )(*args)


def adjoint(tracers, cotangent, east_vel, north_vel, sea_mask, level_count):
    n_trac, lev, rows, cols = tracers.shape
    assert (rows, cols, lev * SLOT) == (ROWS, LANES, LANES)
    n_lon, n_lat = lax.axis_size("lon"), lax.axis_size("lat")
    assert n_lat % 2 == 0
    n_pairs = (n_trac + 1) * lev + 1
    n_fields = 2 * n_trac + 3
    n_sent = -(-n_fields * RIM // SLOT)
    tile = (rows, cols)

    def swap_a(x):
        return lax.ppermute(x, "lat", [(j, j ^ 1) for j in range(n_lat)])

    def swap_b(x):
        pairs = []
        for i in range(n_lon):
            for j in range(n_lat):
                end = j in (0, n_lat - 1)
                to = (i ^ 1, j) if end else (i, ((j + 1) ^ 1) - 1)
                pairs.append((i * n_lat + j, to[0] * n_lat + to[1]))
        return lax.ppermute(x, ("lon", "lat"), pairs)

    def shift(x, by):
        return lax.ppermute(x, "lon", [(i, (i + by) % n_lon) for i in range(n_lon)])

    args = (tracers, cotangent, east_vel, north_vel, sea_mask, level_count)
    args = [pltpu.with_memory_space_constraint(a, pltpu.HBM) for a in args]
    *args, pair_a, pair_b, to_west, to_east, edge = call(
        pack_kernel,
        [jax.ShapeDtypeStruct(a.shape, a.dtype) for a in args]
        + [(n_pairs,) + tile] * 2
        + [(n_sent,) + tile] * 2
        + [(n_fields,) + tile],
        args,
        [pltpu.SemaphoreType.DMA((len(args),))],
        pltpu.HBM,
    )
    from_west = shift(to_east, 1)
    from_east = shift(to_west, -1)
    pair_b = swap_b(pair_b)
    pair_a = swap_a(pair_a)
    corner_a, corner_b = call(corner_kernel, [(n_sent,) + tile] * 2, (from_west, from_east))
    corner_a = swap_a(corner_a)
    corner_b = swap_b(corner_b)
    outs = [tracers.shape, east_vel.shape, north_vel.shape]
    per_plane = (n_trac, lev) + tile
    near = call(
        near_kernel,
        outs + [(STEPS - 1,) + per_plane] * 2 + [(n_trac + 2,) + tile],
        (*args, pair_a),
        [(4,) + per_plane, (STEPS, 2) + per_plane, (len(COEFS), lev, 2) + tile],
    )
    *main, edge_rim = call(
        far_kernel,
        outs + [(n_fields,) + tile],
        (*args, pair_b, *near),
        [(4,) + per_plane, (STEPS, 2) + per_plane, (len(COEFS), lev) + tile, (2, lev) + tile],
    )
    return tuple(
        call(edge_kernel, outs, (edge, edge_rim, from_west, from_east, corner_a, corner_b, *main))
    )


def solution(mesh):
    state, flat, cell = P(None, None, "lat", "lon"), P(None, "lat", "lon"), P("lat", "lon")
    return jax.shard_map(
        adjoint,
        mesh=mesh,
        in_specs=(state, state, flat, flat, cell, cell),
        out_specs=(state, flat, flat),
        check_vma=False,
    )
```

```python
import jax
import jax.numpy as jnp
from jax import lax
from jax.experimental import pallas as pl
from jax.experimental.pallas import tpu as pltpu
from jax.sharding import PartitionSpec as P


STEPS = 4
HORIZ = 0.22
VERT = 0.05

ROWS = 8
LANES = 128
RIM = 4
SLOT = 16
F32 = jnp.float32
VMEM = 8 << 20


def iota(axis):
    return lax.broadcasted_iota(jnp.int32, (ROWS, LANES), axis)


def lane_roll(x, shift):
    shift %= LANES
    return x if shift == 0 else pltpu.roll(x, shift, 1)


def row_roll(x, shift):
    return pltpu.roll(x, shift % ROWS, 0)


def east(x):
    return lane_roll(x, -1)


def west(x):
    return lane_roll(x, 1)


def north(own, rim, last):
    a, b = row_roll(own, -1), row_roll(rim, -1)
    return jnp.where(last, b, a), jnp.where(last, a, b)


def south(own, rim, first):
    a, b = row_roll(own, 1), row_roll(rim, 1)
    return jnp.where(first, b, a), jnp.where(first, a, b)


def odd_row():
    return lax.rem(lax.axis_index("lat"), 2)


def wet_count(mask, count):
    return jnp.where(mask == 1, count, 0).astype(F32)


def edge_of(planes):
    slot = iota(1) // SLOT
    out = None
    for k, plane in enumerate(planes):
        moved = lane_roll(plane, SLOT * k + SLOT // 2)
        out = moved if out is None else jnp.where(slot == k, moved, out)
    return out


def inside_rows(rim):
    place, total = lax.axis_index("lat"), lax.axis_size("lat")
    sub = iota(0)
    keep = ((sub >= RIM) | (place < total - 1)) & ((sub < RIM) | (place > 0))
    return jnp.where(keep, rim, 0.0)


def pack_kernel(*refs):
    args, here, (pair_a, pair_b, to_west, to_east, edge, sems) = refs[:6], refs[6:12], refs[12:]
    copies = [pltpu.make_async_copy(a, b, sems.at[i]) for i, (a, b) in enumerate(zip(args, here))]
    for copy in copies:
        copy.start()
    for copy in copies:
        copy.wait()
    trac, cot, east_vel, north_vel, mask, count = here
    n_trac, lev = trac.shape[:2]
    upper = (iota(0) // RIM) != odd_row()

    def pair(index, p, q):
        q = row_roll(q, RIM)
        pair_a[index] = jnp.where(upper, p, q)
        pair_b[index] = jnp.where(upper, q, p)

    for t in range(n_trac):
        for k in range(lev):
            pair(t * lev + k, trac[t, k], cot[t, k])
    for k in range(lev):
        pair(n_trac * lev + k, east_vel[k], north_vel[k])
    wet = wet_count(mask[...], count[...])
    pair_a[(n_trac + 1) * lev] = wet
    pair_b[(n_trac + 1) * lev] = wet

    fields = [[trac[t, k] for k in range(lev)] for t in range(n_trac)]
    fields += [[cot[t, k] for k in range(lev)] for t in range(n_trac)]
    fields += [[ref[k] for k in range(lev)] for ref in (east_vel, north_vel)]
    fields += [[wet] * lev]
    quarter = (iota(1) % SLOT) // RIM
    west_out, east_out = {}, {}
    for f, planes in enumerate(fields):
        e = edge_of(planes)
        edge[f] = e
        d, g = divmod(f, SLOT // RIM)
        if f == len(fields) - 1 and g == 0:
            west_out[d] = east_out[d] = e
            continue
        moved = lane_roll(e, RIM * g - 8)
        if g == 0:
            west_out[d] = east_out[d] = moved
        else:
            west_out[d] = jnp.where(quarter == g, moved, west_out[d])
            east_out[d] = jnp.where(quarter == g - 1, moved, east_out[d])
    for d in west_out:
        to_west[d] = west_out[d]
        to_east[d] = east_out[d]


def corner_kernel(from_west, from_east, pair_a, pair_b):
    upper = (iota(0) // RIM) != odd_row()
    for d in range(from_west.shape[0]):
        p, q = from_west[d], row_roll(from_east[d], RIM)
        pair_a[d] = jnp.where(upper, p, q)
        pair_b[d] = jnp.where(upper, q, p)


def unpair(a, b):
    from_a = (iota(0) // RIM) == odd_row()
    return jnp.where(from_a, a, b), row_roll(jnp.where(from_a, b, a), RIM)


def velocity_terms(wet, east_wet, north_wet, u, v):
    east_open, north_open = wet * east_wet, wet * north_wet
    hu, hv = 0.5 * u, 0.5 * v
    p, q = east_open * (hu + HORIZ), east_open * (HORIZ - hu)
    r, s = north_open * (hv + HORIZ), north_open * (HORIZ - hv)
    return dict(east_open=east_open, north_open=north_open, p=p, q=q, r=r, s=s, pw=west(p), qw=west(q))


def finish(c, wet, rs, ss, wet_up, wet_down):
    c["rs"], c["ss"] = rs, ss
    centre = wet - ((c["p"] + c["qw"]) + (c["r"] + ss))
    for side, other in (("up", wet_up), ("down", wet_down)):
        if other is not None:
            c[side] = (VERT * wet) * other
            centre = centre - c[side]
    c["centre"] = centre
    return c


def coefficients(wet, wet_up, wet_down, u, v):
    sub = iota(0)
    first, last = sub == 0, sub == ROWS - 1
    north_wet = north(*wet, last)
    out = [velocity_terms(wet[h], east(wet[h]), north_wet[h], u[h], v[h]) for h in range(2)]
    rs, ss = (south(out[0][x], out[1][x], first) for x in "rs")
    for h in range(2):
        finish(out[h], wet[h], rs[h], ss[h], wet_up and wet_up[h], wet_down and wet_down[h])
    return out


FORWARD = ("q", "pw", "s", "rs")
BACKWARD = ("p", "qw", "r", "ss")
COEFS = ("centre", "p", "q", "pw", "qw", "r", "s", "rs", "ss", "up", "down", "east_open", "north_open")


def combine(coef, names, x, e, w, n, s, up, down):
    out = (coef("centre") * x + coef(names[0]) * e) + (coef(names[1]) * w + coef(names[2]) * n)
    out = out + coef(names[3]) * s
    if up is not None:
        out = out + coef("up") * up
    if down is not None:
        out = out + coef("down") * down
    return out


def add(total, term):
    return term if total is None else total + term


def packed_edges(pairs, n_trac, lev):
    groups = [[pairs[i * lev + k] for k in range(lev)] for i in range(n_trac + 1)]
    return [edge_of(g) for g in groups] + [edge_of([pairs[(n_trac + 1) * lev]] * lev)]


def near_kernel(trac, cot, east_vel, north_vel, mask, count, pair_a, adj_t, adj_e, adj_n, past, past_adj, edge_a, rims, sums, coef):
    n_trac, lev = trac.shape[:2]
    sub = iota(0)
    first, last = sub == 0, sub == ROWS - 1
    for i, e in enumerate(packed_edges(pair_a, n_trac, lev)):
        edge_a[i] = e

    def rim(index):
        x = pair_a[index]
        return x, row_roll(x, RIM)

    for t in range(n_trac):
        for k in range(lev):
            rims[0, t, k], rims[2, t, k] = rim(t * lev + k)
    own_side = (sub // RIM) == odd_row()
    count_own = wet_count(mask[...], count[...])
    count_rim = jnp.where(own_side, pair_a[(n_trac + 1) * lev], 0.0)
    wet = [tuple(jnp.where(x > k, 1.0, 0.0) for x in (count_own, count_rim)) for k in range(lev)]
    for k in range(lev):
        u_rim, v_rim = rim(n_trac * lev + k)
        made = coefficients(
            wet[k],
            wet[k + 1] if k + 1 < lev else None,
            wet[k - 1] if k else None,
            (east_vel[k], u_rim),
            (north_vel[k], v_rim),
        )
        for h in range(2):
            for name, value in made[h].items():
                coef[COEFS.index(name), k, h] = value

    def states(own, buf):
        return lambda t, k: (own[t, k], rims[buf, t, k])

    def neighbours(pair):
        own, out = pair
        n, s = north(own, out, last), south(own, out, first)
        return (own, out), (east(own), east(out)), (west(own), west(out)), n, s

    def apply(get, k, t, about, names, h):
        x, e, w, n, s = about
        up = get(t, k + 1)[h] if k + 1 < lev else None
        down = get(t, k - 1)[h] if k else None
        return combine(lambda name: coef[COEFS.index(name), k, h], names, x[h], e[h], w[h], n[h], s[h], up, down)

    for step in range(STEPS):
        get = states(past.at[step - 1] if step else trac, step % 2)
        for k in range(lev):
            for t in range(n_trac):
                if step < STEPS - 1:
                    about = neighbours(get(t, k))
                    past[step, t, k] = apply(get, k, t, about, FORWARD, 0)
                    rims[(step + 1) % 2, t, k] = apply(get, k, t, about, FORWARD, 1)
                    x, e, n = about[0][0], about[1][0], about[3][0]
                else:
                    x, out = get(t, k)
                    e, n = east(x), north(x, out, last)[0]
                sums[step, 0, t, k] = x + e
                sums[step, 1, t, k] = x + n
    for done, step in enumerate(reversed(range(STEPS))):
        get = states(past_adj.at[done - 1] if done else cot, 2 + done % 2)
        for k in range(lev):
            acc_e = acc_n = None
            for t in range(n_trac):
                about = neighbours(get(t, k))
                new = apply(get, k, t, about, BACKWARD, 0)
                if step:
                    past_adj[done, t, k] = new
                    rims[2 + (done + 1) % 2, t, k] = apply(get, k, t, about, BACKWARD, 1)
                else:
                    adj_t[t, k] = new
                x, e, n = about[0][0], about[1][0], about[3][0]
                acc_e = add(acc_e, sums[step, 0, t, k] * (e - x))
                acc_n = add(acc_n, sums[step, 1, t, k] * (n - x))
            if done:
                acc_e, acc_n = acc_e + adj_e[k], acc_n + adj_n[k]
            if step == 0:
                acc_e = acc_e * (0.5 * coef[COEFS.index("east_open"), k, 0])
                acc_n = acc_n * (0.5 * coef[COEFS.index("north_open"), k, 0])
            adj_e[k] = acc_e
            adj_n[k] = acc_n


def march(steps):
    for i in range(steps):
        yield lambda part: part.backward(i)
        yield lambda part: part.forward(i)
        for step in range(steps):
            if max(step, steps - 1 - step) == i:
                yield lambda part: part.collect(step)


class Far:
    def __init__(self, args, pair_b, past, past_adj, state, sums, slopes, coef, acc):
        self.slopes, self.started = slopes, False
        self.trac, self.cot, east_vel, north_vel, mask, count = args
        self.past, self.past_adj, self.state, self.sums, self.coef, self.acc = past, past_adj, state, sums, coef, acc
        n_trac, lev = self.n_trac, self.lev = self.trac.shape[:2]
        sub = iota(0)
        self.first, self.last = sub == 0, sub == ROWS - 1
        self.rim = (sub // RIM) == odd_row()

        def both(index, p, q):
            x = pair_b[index]
            return self.join(row_roll(x, RIM), p), self.join(x, q)

        for t in range(n_trac):
            for k in range(lev):
                state[0, t, k], state[2, t, k] = both(t * lev + k, self.trac[t, k], self.cot[t, k])
        place = lax.axis_index("lat")
        outside = (place == 0) | (place == lax.axis_size("lat") - 1)
        count_own = wet_count(mask[...], count[...])
        count_rim = row_roll(pair_b[(n_trac + 1) * lev], RIM)
        count_far = self.join(jnp.where(outside, jnp.zeros_like(count_rim), count_rim), count_own)
        own = [jnp.where(count_own > k, 1.0, 0.0) for k in range(lev)]
        far = [jnp.where(count_far > k, 1.0, 0.0) for k in range(lev)]
        for k in range(lev):
            u, v = both(n_trac * lev + k, east_vel[k], north_vel[k])
            beyond = velocity_terms(own[k], own[k], row_roll(own[k], -1), north_vel[k], north_vel[k])
            made = velocity_terms(far[k], east(far[k]), self.north(far[k], own[k]), u, v)
            rs, ss = (self.south(made[x], beyond[x]) for x in "rs")
            finish(made, far[k], rs, ss, far[k + 1] if k + 1 < lev else None, far[k - 1] if k else None)
            for name, value in made.items():
                coef[COEFS.index(name), k] = value

    def join(self, rim, own):
        return jnp.where(self.rim, rim, row_roll(own, RIM))

    def north(self, x, beyond):
        return jnp.where(self.last, row_roll(beyond, 3), row_roll(x, -1))

    def south(self, x, beyond):
        return jnp.where(self.first, row_roll(beyond, -3), row_roll(x, 1))

    def apply(self, buf, t, k, about, names):
        up = self.state[buf, t, k + 1] if k + 1 < self.lev else None
        down = self.state[buf, t, k - 1] if k else None
        return combine(lambda name: self.coef[COEFS.index(name), k], names, *about, up, down)

    def forward(self, step):
        src, dst = step % 2, (step + 1) % 2
        own = self.past.at[step - 1] if step else self.trac
        for k in range(self.lev):
            for t in range(self.n_trac):
                x, beyond = self.state[src, t, k], own[t, k]
                e, n = east(x), self.north(x, beyond)
                self.sums[step, 0, t, k] = x + e
                self.sums[step, 1, t, k] = x + n
                if step < STEPS - 1:
                    about = x, e, west(x), n, self.south(x, beyond)
                    self.state[dst, t, k] = self.apply(src, t, k, about, FORWARD)

    def backward(self, done):
        step = STEPS - 1 - done
        src, dst = 2 + done % 2, 2 + (done + 1) % 2
        own = self.past_adj.at[done - 1] if done else self.cot
        for k in range(self.lev):
            for t in range(self.n_trac):
                x, beyond = self.state[src, t, k], own[t, k]
                e, n = east(x), self.north(x, beyond)
                about = x, e, west(x), n, self.south(x, beyond)
                self.state[dst, t, k] = self.apply(src, t, k, about, BACKWARD)
                self.slopes[step, 0, t, k] = e - x
                self.slopes[step, 1, t, k] = n - x

    def collect(self, step):
        for k in range(self.lev):
            for i in range(2):
                total = self.acc[i, k] if self.started else None
                for t in range(self.n_trac):
                    total = add(total, self.sums[step, i, t, k] * self.slopes[step, i, t, k])
                self.acc[i, k] = total
        self.started = True

    def merged(self, t, k, near):
        return jnp.where(self.rim, row_roll(self.state[2 + STEPS % 2, t, k], RIM), near)

    def merged_gradient(self, i, k, near):
        opened = self.coef[COEFS.index(("east_open", "north_open")[i]), k]
        return jnp.where(self.rim, row_roll(self.acc[i, k] * (0.5 * opened), RIM), near)


class Strip:
    def __init__(self, side, n_trac, lev, edge, rims, sent, corners):
        self.n_trac = n_trac
        n_fields = edge.shape[0]
        sub, lane = iota(0), iota(1)
        self.first, self.last = sub == 0, sub == ROWS - 1
        level = lane // SLOT
        from_side = (lane % SLOT) // RIM == 1 + side

        def field(f):
            d, g = divmod(f, SLOT // RIM)
            shift = 0 if f == n_fields - 1 and g == 0 else 8 - RIM * g
            own = jnp.where(from_side, lane_roll(sent[d], shift), edge[f])
            rim = jnp.where(from_side, lane_roll(corners[d], shift), rims[f])
            return own, rim

        own, rim = field(n_fields - 1)
        levels = level.astype(F32)
        wet = tuple(jnp.where(x > levels, 1.0, 0.0) for x in (own, inside_rows(rim)))
        up = tuple(jnp.where(level < lev - 1, lane_roll(x, -SLOT), 0.0) for x in wet)
        down = tuple(jnp.where(level > 0, lane_roll(x, SLOT), 0.0) for x in wet)
        self.made = coefficients(wet, up, down, field(2 * n_trac), field(2 * n_trac + 1))
        self.state = [field(t) for t in range(n_trac)]
        self.lam = [field(n_trac + t) for t in range(n_trac)]
        self.sums, self.slopes, self.acc_e, self.acc_n = [], {}, None, None

    def near(self, x):
        n, s = north(*x, self.last), south(*x, self.first)
        return x, tuple(map(east, x)), tuple(map(west, x)), n, s

    def apply(self, about, names, halves):
        x, e, w, n, s = about
        return tuple(
            combine(self.made[h].__getitem__, names, x[h], e[h], w[h], n[h], s[h], lane_roll(x[h], -SLOT), lane_roll(x[h], SLOT))
            for h in halves
        )

    def forward(self, step):
        about = [self.near(x) for x in self.state]
        self.sums.append([(a[0][0] + a[1][0], a[0][0] + a[3][0]) for a in about])
        if step < STEPS - 1:
            self.state = [self.apply(a, FORWARD, (0, 1)) for a in about]

    def backward(self, done):
        step = STEPS - 1 - done
        about = [self.near(x) for x in self.lam]
        self.slopes[step] = [(a[1][0] - a[0][0], a[3][0] - a[0][0]) for a in about]
        self.lam = [self.apply(a, BACKWARD, (0, 1) if step else (0,)) for a in about]

    def collect(self, step):
        for (sum_e, sum_n), (slope_e, slope_n) in zip(self.sums[step], self.slopes[step]):
            self.acc_e = add(self.acc_e, sum_e * slope_e)
            self.acc_n = add(self.acc_n, sum_n * slope_n)

    def gradients(self):
        own = self.made[0]
        return self.acc_e * (0.5 * own["east_open"]), self.acc_n * (0.5 * own["north_open"])


def far_kernel(*refs):
    args, refs = refs[:6], refs[6:]
    pair_b, near_t, near_e, near_n, past, past_adj, edge_a = refs[:7]
    adj_t, adj_e, adj_n, edge_rim, state, sums, slopes, coef, acc = refs[7:]
    n_trac, lev = near_t.shape[:2]

    for i, b in enumerate(packed_edges(pair_b, n_trac, lev)):
        p, q = unpair(edge_a[i], b)
        if i < n_trac:
            edge_rim[i], edge_rim[n_trac + i] = p, q
        elif i == n_trac:
            edge_rim[2 * n_trac], edge_rim[2 * n_trac + 1] = p, q
        else:
            edge_rim[2 * n_trac + 2] = p
    far = Far(args, pair_b, past, past_adj, state, sums, slopes, coef, acc)
    for part in march(STEPS):
        part(far)
    for k in range(lev):
        for t in range(n_trac):
            adj_t[t, k] = far.merged(t, k, near_t[t, k])
        adj_e[k] = far.merged_gradient(0, k, near_e[k])
        adj_n[k] = far.merged_gradient(1, k, near_n[k])


def edge_kernel(edge, edge_rim, from_west, from_east, corner_a, corner_b, main_t, main_e, main_n, adj_t, adj_e, adj_n):
    n_trac, lev = main_t.shape[:2]
    corners = [unpair(corner_a[d], corner_b[d]) for d in range(from_west.shape[0])]
    strips = [
        Strip(side, n_trac, lev, edge, edge_rim, sent, [c[side] for c in corners])
        for side, sent in enumerate((from_west, from_east))
    ]
    for part in march(STEPS):
        for strip in strips:
            part(strip)

    lane = iota(1)
    at_west = (lane % SLOT) // RIM >= 2
    margin = (lane < RIM) | (lane >= LANES - RIM)

    def put(ref, index, k, both, main):
        ref[index] = jnp.where(margin, lane_roll(both, -(SLOT * k + SLOT // 2)), main[index])

    for t in range(n_trac):
        both = jnp.where(at_west, strips[0].lam[t][0], strips[1].lam[t][0])
        for k in range(lev):
            put(adj_t, (t, k), k, both, main_t)
    for ref, main, *sides in zip((adj_e, adj_n), (main_e, main_n), *(s.gradients() for s in strips)):
        both = jnp.where(at_west, *sides)
        for k in range(lev):
            put(ref, (k,), k, both, main)


def call(body, outs, args, scratch=(), space=pltpu.VMEM):
    shapes = [s if hasattr(s, "dtype") else jax.ShapeDtypeStruct(s, F32) for s in outs]
    return pl.pallas_call(
        body,
        out_shape=shapes,
        in_specs=[pl.BlockSpec(memory_space=space)] * len(args),
        out_specs=[pl.BlockSpec(memory_space=pltpu.VMEM)] * len(outs),
        scratch_shapes=[pltpu.VMEM(s, F32) if isinstance(s, tuple) else s for s in scratch],
        compiler_params=pltpu.CompilerParams(vmem_limit_bytes=VMEM),
    )(*args)


def adjoint(tracers, cotangent, east_vel, north_vel, sea_mask, level_count):
    n_trac, lev, rows, cols = tracers.shape
    assert (rows, cols, lev * SLOT) == (ROWS, LANES, LANES)
    n_lon, n_lat = lax.axis_size("lon"), lax.axis_size("lat")
    assert n_lat % 2 == 0
    n_pairs = (n_trac + 1) * lev + 1
    n_fields = 2 * n_trac + 3
    n_sent = -(-n_fields * RIM // SLOT)
    tile = (rows, cols)

    def swap_a(x):
        return lax.ppermute(x, "lat", [(j, j ^ 1) for j in range(n_lat)])

    def swap_b(x):
        pairs = []
        for i in range(n_lon):
            for j in range(n_lat):
                end = j in (0, n_lat - 1)
                to = (i ^ 1, j) if end else (i, ((j + 1) ^ 1) - 1)
                pairs.append((i * n_lat + j, to[0] * n_lat + to[1]))
        return lax.ppermute(x, ("lon", "lat"), pairs)

    def shift(x, by):
        return lax.ppermute(x, "lon", [(i, (i + by) % n_lon) for i in range(n_lon)])

    args = (tracers, cotangent, east_vel, north_vel, sea_mask, level_count)
    args = [pltpu.with_memory_space_constraint(a, pltpu.HBM) for a in args]
    *args, pair_a, pair_b, to_west, to_east, edge = call(
        pack_kernel,
        [jax.ShapeDtypeStruct(a.shape, a.dtype) for a in args]
        + [(n_pairs,) + tile] * 2
        + [(n_sent,) + tile] * 2
        + [(n_fields,) + tile],
        args,
        [pltpu.SemaphoreType.DMA((len(args),))],
        pltpu.HBM,
    )
    from_west = shift(to_east, 1)
    from_east = shift(to_west, -1)
    pair_b = swap_b(pair_b)
    corner_a, corner_b = call(corner_kernel, [(n_sent,) + tile] * 2, (from_west, from_east))
    both_a = swap_a(jnp.concatenate([pair_a, corner_a]))
    pair_a, corner_a = both_a, both_a[n_pairs:]
    corner_b = swap_b(corner_b)
    outs = [tracers.shape, east_vel.shape, north_vel.shape]
    per_plane = (n_trac, lev) + tile
    near = call(
        near_kernel,
        outs + [(STEPS - 1,) + per_plane] * 2 + [(n_trac + 2,) + tile],
        (*args, pair_a),
        [(4,) + per_plane, (STEPS, 2) + per_plane, (len(COEFS), lev, 2) + tile],
    )
    *main, edge_rim = call(
        far_kernel,
        outs + [(n_fields,) + tile],
        (*args, pair_b, *near),
        [(4,) + per_plane] + [(STEPS, 2) + per_plane] * 2 + [(len(COEFS), lev) + tile, (2, lev) + tile],
    )
    return tuple(
        call(edge_kernel, outs, (edge, edge_rim, from_west, from_east, corner_a, corner_b, *main))
    )


def solution(mesh):
    state, flat, cell = P(None, None, "lat", "lon"), P(None, "lat", "lon"), P("lat", "lon")
    return jax.shard_map(
        adjoint,
        mesh=mesh,
        in_specs=(state, state, flat, flat, cell, cell),
        out_specs=(state, flat, flat),
        check_vma=False,
    )
```

```python
import jax
import jax.numpy as jnp
from jax import lax
from jax.experimental import pallas as pl
from jax.experimental.pallas import tpu as pltpu
from jax.sharding import PartitionSpec as P


STEPS = 4
HORIZ = 0.22
VERT = 0.05

ROWS = 8
LANES = 128
RIM = 4
SLOT = 16
F32 = jnp.float32
VMEM = 8 << 20


def iota(axis):
    return lax.broadcasted_iota(jnp.int32, (ROWS, LANES), axis)


def lane_roll(x, shift):
    shift %= LANES
    return x if shift == 0 else pltpu.roll(x, shift, 1)


def row_roll(x, shift):
    return pltpu.roll(x, shift % ROWS, 0)


def east(x):
    return lane_roll(x, -1)


def west(x):
    return lane_roll(x, 1)


def north(own, rim, last):
    a, b = row_roll(own, -1), row_roll(rim, -1)
    return jnp.where(last, b, a), jnp.where(last, a, b)


def south(own, rim, first):
    a, b = row_roll(own, 1), row_roll(rim, 1)
    return jnp.where(first, b, a), jnp.where(first, a, b)


def odd_row():
    return lax.rem(lax.axis_index("lat"), 2)


def wet_count(mask, count):
    return jnp.where(mask == 1, count, 0).astype(F32)


def edge_of(planes):
    slot = iota(1) // SLOT
    out = None
    for k, plane in enumerate(planes):
        moved = lane_roll(plane, SLOT * k + SLOT // 2)
        out = moved if out is None else jnp.where(slot == k, moved, out)
    return out


def inside_rows(rim):
    place, total = lax.axis_index("lat"), lax.axis_size("lat")
    sub = iota(0)
    keep = ((sub >= RIM) | (place < total - 1)) & ((sub < RIM) | (place > 0))
    return jnp.where(keep, rim, 0.0)


def pack_kernel(*refs):
    args, here, (pair_a, pair_b, to_west, to_east, edge, sems) = refs[:6], refs[6:12], refs[12:]
    parts = [(a.at[t], b.at[t]) for a, b in zip(args[:2], here[:2]) for t in range(a.shape[0])]
    parts += list(zip(args[2:], here[2:]))
    copies = [pltpu.make_async_copy(a, b, sems.at[i]) for i, (a, b) in enumerate(parts)]
    for copy in copies:
        copy.start()
    for copy in copies:
        copy.wait()
    trac, cot, east_vel, north_vel, mask, count = here
    n_trac, lev = trac.shape[:2]
    upper = (iota(0) // RIM) != odd_row()

    def pair(index, p, q):
        q = row_roll(q, RIM)
        pair_a[index] = jnp.where(upper, p, q)
        pair_b[index] = jnp.where(upper, q, p)

    for t in range(n_trac):
        for k in range(lev):
            pair(t * lev + k, trac[t, k], cot[t, k])
    for k in range(lev):
        pair(n_trac * lev + k, east_vel[k], north_vel[k])
    wet = wet_count(mask[...], count[...])
    pair_a[(n_trac + 1) * lev] = wet
    pair_b[(n_trac + 1) * lev] = wet

    fields = [[trac[t, k] for k in range(lev)] for t in range(n_trac)]
    fields += [[cot[t, k] for k in range(lev)] for t in range(n_trac)]
    fields += [[ref[k] for k in range(lev)] for ref in (east_vel, north_vel)]
    fields += [[wet] * lev]
    quarter = (iota(1) % SLOT) // RIM
    west_out, east_out = {}, {}
    for f, planes in enumerate(fields):
        e = edge_of(planes)
        edge[f] = e
        d, g = divmod(f, SLOT // RIM)
        if f == len(fields) - 1 and g == 0:
            west_out[d] = east_out[d] = e
            continue
        moved = lane_roll(e, RIM * g - 8)
        if g == 0:
            west_out[d] = east_out[d] = moved
        else:
            west_out[d] = jnp.where(quarter == g, moved, west_out[d])
            east_out[d] = jnp.where(quarter == g - 1, moved, east_out[d])
    for d in west_out:
        to_west[d] = west_out[d]
        to_east[d] = east_out[d]


def corner_kernel(from_west, from_east, pair_a, pair_b):
    upper = (iota(0) // RIM) != odd_row()
    for d in range(from_west.shape[0]):
        p, q = from_west[d], row_roll(from_east[d], RIM)
        pair_a[d] = jnp.where(upper, p, q)
        pair_b[d] = jnp.where(upper, q, p)


def unpair(a, b):
    from_a = (iota(0) // RIM) == odd_row()
    return jnp.where(from_a, a, b), row_roll(jnp.where(from_a, b, a), RIM)


def velocity_terms(wet, east_wet, north_wet, u, v):
    east_open, north_open = wet * east_wet, wet * north_wet
    hu, hv = 0.5 * u, 0.5 * v
    p, q = east_open * (hu + HORIZ), east_open * (HORIZ - hu)
    r, s = north_open * (hv + HORIZ), north_open * (HORIZ - hv)
    return dict(east_open=east_open, north_open=north_open, p=p, q=q, r=r, s=s, pw=west(p), qw=west(q))


def finish(c, wet, rs, ss, wet_up, wet_down):
    c["rs"], c["ss"] = rs, ss
    centre = wet - ((c["p"] + c["qw"]) + (c["r"] + ss))
    for side, other in (("up", wet_up), ("down", wet_down)):
        if other is not None:
            c[side] = (VERT * wet) * other
            centre = centre - c[side]
    c["centre"] = centre
    return c


def coefficients(wet, wet_up, wet_down, u, v):
    sub = iota(0)
    first, last = sub == 0, sub == ROWS - 1
    north_wet = north(*wet, last)
    out = [velocity_terms(wet[h], east(wet[h]), north_wet[h], u[h], v[h]) for h in range(2)]
    rs, ss = (south(out[0][x], out[1][x], first) for x in "rs")
    for h in range(2):
        finish(out[h], wet[h], rs[h], ss[h], wet_up and wet_up[h], wet_down and wet_down[h])
    return out


FORWARD = ("q", "pw", "s", "rs")
BACKWARD = ("p", "qw", "r", "ss")
COEFS = ("centre", "p", "q", "pw", "qw", "r", "s", "rs", "ss", "up", "down", "east_open", "north_open")


def combine(coef, names, x, e, w, n, s, up, down):
    out = (coef("centre") * x + coef(names[0]) * e) + (coef(names[1]) * w + coef(names[2]) * n)
    out = out + coef(names[3]) * s
    if up is not None:
        out = out + coef("up") * up
    if down is not None:
        out = out + coef("down") * down
    return out


def add(total, term):
    return term if total is None else total + term


def packed_edges(pairs, n_trac, lev):
    groups = [[pairs[i * lev + k] for k in range(lev)] for i in range(n_trac + 1)]
    return [edge_of(g) for g in groups] + [edge_of([pairs[(n_trac + 1) * lev]] * lev)]


def near_kernel(trac, cot, east_vel, north_vel, mask, count, pair_a, adj_t, adj_e, adj_n, past, past_adj, edge_a, rims, sums, coef):
    n_trac, lev = trac.shape[:2]
    sub = iota(0)
    first, last = sub == 0, sub == ROWS - 1
    for i, e in enumerate(packed_edges(pair_a, n_trac, lev)):
        edge_a[i] = e

    def rim(index):
        x = pair_a[index]
        return x, row_roll(x, RIM)

    for t in range(n_trac):
        for k in range(lev):
            rims[0, t, k], rims[2, t, k] = rim(t * lev + k)
    own_side = (sub // RIM) == odd_row()
    count_own = wet_count(mask[...], count[...])
    count_rim = jnp.where(own_side, pair_a[(n_trac + 1) * lev], 0.0)
    wet = [tuple(jnp.where(x > k, 1.0, 0.0) for x in (count_own, count_rim)) for k in range(lev)]
    for k in range(lev):
        u_rim, v_rim = rim(n_trac * lev + k)
        made = coefficients(
            wet[k],
            wet[k + 1] if k + 1 < lev else None,
            wet[k - 1] if k else None,
            (east_vel[k], u_rim),
            (north_vel[k], v_rim),
        )
        for h in range(2):
            for name, value in made[h].items():
                coef[COEFS.index(name), k, h] = value

    def states(own, buf):
        return lambda t, k: (own[t, k], rims[buf, t, k])

    def neighbours(pair):
        own, out = pair
        n, s = north(own, out, last), south(own, out, first)
        return (own, out), (east(own), east(out)), (west(own), west(out)), n, s

    def apply(get, k, t, about, names, h):
        x, e, w, n, s = about
        up = get(t, k + 1)[h] if k + 1 < lev else None
        down = get(t, k - 1)[h] if k else None
        return combine(lambda name: coef[COEFS.index(name), k, h], names, x[h], e[h], w[h], n[h], s[h], up, down)

    for step in range(STEPS):
        get = states(past.at[step - 1] if step else trac, step % 2)
        for k in range(lev):
            for t in range(n_trac):
                if step < STEPS - 1:
                    about = neighbours(get(t, k))
                    past[step, t, k] = apply(get, k, t, about, FORWARD, 0)
                    rims[(step + 1) % 2, t, k] = apply(get, k, t, about, FORWARD, 1)
                    x, e, n = about[0][0], about[1][0], about[3][0]
                else:
                    x, out = get(t, k)
                    e, n = east(x), north(x, out, last)[0]
                sums[step, 0, t, k] = x + e
                sums[step, 1, t, k] = x + n
    for done, step in enumerate(reversed(range(STEPS))):
        get = states(past_adj.at[done - 1] if done else cot, 2 + done % 2)
        for k in range(lev):
            acc_e = acc_n = None
            for t in range(n_trac):
                about = neighbours(get(t, k))
                new = apply(get, k, t, about, BACKWARD, 0)
                if step:
                    past_adj[done, t, k] = new
                    rims[2 + (done + 1) % 2, t, k] = apply(get, k, t, about, BACKWARD, 1)
                else:
                    adj_t[t, k] = new
                x, e, n = about[0][0], about[1][0], about[3][0]
                acc_e = add(acc_e, sums[step, 0, t, k] * (e - x))
                acc_n = add(acc_n, sums[step, 1, t, k] * (n - x))
            if done:
                acc_e, acc_n = acc_e + adj_e[k], acc_n + adj_n[k]
            if step == 0:
                acc_e = acc_e * (0.5 * coef[COEFS.index("east_open"), k, 0])
                acc_n = acc_n * (0.5 * coef[COEFS.index("north_open"), k, 0])
            adj_e[k] = acc_e
            adj_n[k] = acc_n


def march(steps):
    for i in range(steps):
        yield lambda part: part.backward(i)
        yield lambda part: part.forward(i)
        for step in range(steps):
            if max(step, steps - 1 - step) == i:
                yield lambda part: part.collect(step)


def beyond_kernel(trac, cot, past, past_adj, beyond, beside):
    first = iota(0) == 0
    n_trac, lev = trac.shape[:2]
    for i, (start, later) in enumerate(((trac, past), (cot, past_adj))):
        for t in range(n_trac):
            for k in range(lev):
                beside[i, t, k] = row_roll(start[t, k], RIM)
                for step in range(STEPS):
                    x = later[step - 1, t, k] if step else start[t, k]
                    beyond[i, step, t, k] = jnp.where(first, row_roll(x, -3), row_roll(x, 3))


class Far:
    def __init__(self, args, pair_b, beyond, beside, state, sums, slopes, coef, acc):
        self.slopes, self.started = slopes, False
        self.trac, self.cot, east_vel, north_vel, mask, count = args
        self.beyond, self.state, self.sums, self.coef, self.acc = beyond, state, sums, coef, acc
        n_trac, lev = self.n_trac, self.lev = self.trac.shape[:2]
        sub = iota(0)
        self.first, self.last = sub == 0, sub == ROWS - 1
        self.rim = (sub // RIM) == odd_row()

        def both(index, p, q):
            x = pair_b[index]
            return jnp.where(self.rim, row_roll(x, RIM), p), jnp.where(self.rim, x, q)

        for t in range(n_trac):
            for k in range(lev):
                state[0, t, k], state[2, t, k] = both(t * lev + k, beside[0, t, k], beside[1, t, k])
        place = lax.axis_index("lat")
        outside = (place == 0) | (place == lax.axis_size("lat") - 1)
        count_own = wet_count(mask[...], count[...])
        count_rim = row_roll(pair_b[(n_trac + 1) * lev], RIM)
        count_far = self.join(jnp.where(outside, jnp.zeros_like(count_rim), count_rim), count_own)
        own = [jnp.where(count_own > k, 1.0, 0.0) for k in range(lev)]
        far = [jnp.where(count_far > k, 1.0, 0.0) for k in range(lev)]
        for k in range(lev):
            u, v = both(n_trac * lev + k, row_roll(east_vel[k], RIM), row_roll(north_vel[k], RIM))
            beyond = velocity_terms(own[k], own[k], row_roll(own[k], -1), north_vel[k], north_vel[k])
            made = velocity_terms(far[k], east(far[k]), self.north(far[k], own[k]), u, v)
            rs, ss = (self.south(made[x], beyond[x]) for x in "rs")
            finish(made, far[k], rs, ss, far[k + 1] if k + 1 < lev else None, far[k - 1] if k else None)
            for name, value in made.items():
                coef[COEFS.index(name), k] = value

    def join(self, rim, own):
        return jnp.where(self.rim, rim, row_roll(own, RIM))

    def north(self, x, beyond):
        return jnp.where(self.last, row_roll(beyond, 3), row_roll(x, -1))

    def south(self, x, beyond):
        return jnp.where(self.first, row_roll(beyond, -3), row_roll(x, 1))

    def next_row(self, x, beyond):
        return jnp.where(self.last, beyond, row_roll(x, -1))

    def row_before(self, x, beyond):
        return jnp.where(self.first, beyond, row_roll(x, 1))

    def apply(self, buf, t, k, about, names):
        up = self.state[buf, t, k + 1] if k + 1 < self.lev else None
        down = self.state[buf, t, k - 1] if k else None
        return combine(lambda name: self.coef[COEFS.index(name), k], names, *about, up, down)

    def forward(self, step):
        src, dst = step % 2, (step + 1) % 2
        for k in range(self.lev):
            for t in range(self.n_trac):
                x, beyond = self.state[src, t, k], self.beyond[0, step, t, k]
                e, n = east(x), self.next_row(x, beyond)
                self.sums[step, 0, t, k] = x + e
                self.sums[step, 1, t, k] = x + n
                if step < STEPS - 1:
                    about = x, e, west(x), n, self.row_before(x, beyond)
                    self.state[dst, t, k] = self.apply(src, t, k, about, FORWARD)

    def backward(self, done):
        step = STEPS - 1 - done
        src, dst = 2 + done % 2, 2 + (done + 1) % 2
        for k in range(self.lev):
            for t in range(self.n_trac):
                x, beyond = self.state[src, t, k], self.beyond[1, done, t, k]
                e, n = east(x), self.next_row(x, beyond)
                about = x, e, west(x), n, self.row_before(x, beyond)
                self.state[dst, t, k] = self.apply(src, t, k, about, BACKWARD)
                self.slopes[step, 0, t, k] = e - x
                self.slopes[step, 1, t, k] = n - x

    def collect(self, step):
        for k in range(self.lev):
            for i in range(2):
                total = self.acc[i, k] if self.started else None
                for t in range(self.n_trac):
                    total = add(total, self.sums[step, i, t, k] * self.slopes[step, i, t, k])
                self.acc[i, k] = total
        self.started = True

    def merged(self, t, k, near):
        return jnp.where(self.rim, row_roll(self.state[2 + STEPS % 2, t, k], RIM), near)

    def merged_gradient(self, i, k, near):
        opened = self.coef[COEFS.index(("east_open", "north_open")[i]), k]
        return jnp.where(self.rim, row_roll(self.acc[i, k] * (0.5 * opened), RIM), near)


class Strip:
    def __init__(self, side, n_trac, lev, edge, rims, sent, corners):
        self.n_trac = n_trac
        n_fields = edge.shape[0]
        sub, lane = iota(0), iota(1)
        self.first, self.last = sub == 0, sub == ROWS - 1
        level = lane // SLOT
        from_side = (lane % SLOT) // RIM == 1 + side

        def field(f):
            d, g = divmod(f, SLOT // RIM)
            shift = 0 if f == n_fields - 1 and g == 0 else 8 - RIM * g
            own = jnp.where(from_side, lane_roll(sent[d], shift), edge[f])
            rim = jnp.where(from_side, lane_roll(corners[d], shift), rims[f])
            return own, rim

        own, rim = field(n_fields - 1)
        levels = level.astype(F32)
        wet = tuple(jnp.where(x > levels, 1.0, 0.0) for x in (own, inside_rows(rim)))
        up = tuple(jnp.where(level < lev - 1, lane_roll(x, -SLOT), 0.0) for x in wet)
        down = tuple(jnp.where(level > 0, lane_roll(x, SLOT), 0.0) for x in wet)
        self.made = coefficients(wet, up, down, field(2 * n_trac), field(2 * n_trac + 1))
        self.state = [field(t) for t in range(n_trac)]
        self.lam = [field(n_trac + t) for t in range(n_trac)]
        self.sums, self.slopes, self.acc_e, self.acc_n = [], {}, None, None

    def near(self, x):
        n, s = north(*x, self.last), south(*x, self.first)
        return x, tuple(map(east, x)), tuple(map(west, x)), n, s

    def apply(self, about, names, halves):
        x, e, w, n, s = about
        return tuple(
            combine(self.made[h].__getitem__, names, x[h], e[h], w[h], n[h], s[h], lane_roll(x[h], -SLOT), lane_roll(x[h], SLOT))
            for h in halves
        )

    def forward(self, step):
        about = [self.near(x) for x in self.state]
        self.sums.append([(a[0][0] + a[1][0], a[0][0] + a[3][0]) for a in about])
        if step < STEPS - 1:
            self.state = [self.apply(a, FORWARD, (0, 1)) for a in about]

    def backward(self, done):
        step = STEPS - 1 - done
        about = [self.near(x) for x in self.lam]
        self.slopes[step] = [(a[1][0] - a[0][0], a[3][0] - a[0][0]) for a in about]
        self.lam = [self.apply(a, BACKWARD, (0, 1) if step else (0,)) for a in about]

    def collect(self, step):
        for (sum_e, sum_n), (slope_e, slope_n) in zip(self.sums[step], self.slopes[step]):
            self.acc_e = add(self.acc_e, sum_e * slope_e)
            self.acc_n = add(self.acc_n, sum_n * slope_n)

    def gradients(self):
        own = self.made[0]
        return self.acc_e * (0.5 * own["east_open"]), self.acc_n * (0.5 * own["north_open"])


def far_kernel(*refs):
    args, refs = refs[:6], refs[6:]
    pair_b, near_t, near_e, near_n, edge_a, beyond, beside = refs[:7]
    adj_t, adj_e, adj_n, edge_rim, state, sums, slopes, coef, acc = refs[7:]
    n_trac, lev = near_t.shape[:2]

    for i, b in enumerate(packed_edges(pair_b, n_trac, lev)):
        p, q = unpair(edge_a[i], b)
        if i < n_trac:
            edge_rim[i], edge_rim[n_trac + i] = p, q
        elif i == n_trac:
            edge_rim[2 * n_trac], edge_rim[2 * n_trac + 1] = p, q
        else:
            edge_rim[2 * n_trac + 2] = p
    far = Far(args, pair_b, beyond, beside, state, sums, slopes, coef, acc)
    for part in march(STEPS):
        part(far)
    for k in range(lev):
        for t in range(n_trac):
            adj_t[t, k] = far.merged(t, k, near_t[t, k])
        adj_e[k] = far.merged_gradient(0, k, near_e[k])
        adj_n[k] = far.merged_gradient(1, k, near_n[k])


def edge_kernel(edge, edge_rim, from_west, from_east, corner_a, corner_b, main_t, main_e, main_n, adj_t, adj_e, adj_n):
    n_trac, lev = main_t.shape[:2]
    corners = [unpair(corner_a[d], corner_b[d]) for d in range(from_west.shape[0])]
    strips = [
        Strip(side, n_trac, lev, edge, edge_rim, sent, [c[side] for c in corners])
        for side, sent in enumerate((from_west, from_east))
    ]
    for part in march(STEPS):
        for strip in strips:
            part(strip)

    lane = iota(1)
    at_west = (lane % SLOT) // RIM >= 2
    margin = (lane < RIM) | (lane >= LANES - RIM)

    def put(ref, index, k, both, main):
        ref[index] = jnp.where(margin, lane_roll(both, -(SLOT * k + SLOT // 2)), main[index])

    for t in range(n_trac):
        both = jnp.where(at_west, strips[0].lam[t][0], strips[1].lam[t][0])
        for k in range(lev):
            put(adj_t, (t, k), k, both, main_t)
    for ref, main, *sides in zip((adj_e, adj_n), (main_e, main_n), *(s.gradients() for s in strips)):
        both = jnp.where(at_west, *sides)
        for k in range(lev):
            put(ref, (k,), k, both, main)


def call(body, outs, args, scratch=(), space=pltpu.VMEM):
    shapes = [s if hasattr(s, "dtype") else jax.ShapeDtypeStruct(s, F32) for s in outs]
    return pl.pallas_call(
        body,
        out_shape=shapes,
        in_specs=[pl.BlockSpec(memory_space=space)] * len(args),
        out_specs=[pl.BlockSpec(memory_space=pltpu.VMEM)] * len(outs),
        scratch_shapes=[pltpu.VMEM(s, F32) if isinstance(s, tuple) else s for s in scratch],
        compiler_params=pltpu.CompilerParams(vmem_limit_bytes=VMEM),
    )(*args)


def adjoint(tracers, cotangent, east_vel, north_vel, sea_mask, level_count):
    n_trac, lev, rows, cols = tracers.shape
    assert (rows, cols, lev * SLOT) == (ROWS, LANES, LANES)
    n_lon, n_lat = lax.axis_size("lon"), lax.axis_size("lat")
    assert n_lat % 2 == 0
    n_pairs = (n_trac + 1) * lev + 1
    n_fields = 2 * n_trac + 3
    n_sent = -(-n_fields * RIM // SLOT)
    tile = (rows, cols)

    def swap_a(x):
        return lax.ppermute(x, "lat", [(j, j ^ 1) for j in range(n_lat)])

    def swap_b(x):
        pairs = []
        for i in range(n_lon):
            for j in range(n_lat):
                end = j in (0, n_lat - 1)
                to = (i ^ 1, j) if end else (i, ((j + 1) ^ 1) - 1)
                pairs.append((i * n_lat + j, to[0] * n_lat + to[1]))
        return lax.ppermute(x, ("lon", "lat"), pairs)

    def shift(x, by):
        return lax.ppermute(x, "lon", [(i, (i + by) % n_lon) for i in range(n_lon)])

    args = (tracers, cotangent, east_vel, north_vel, sea_mask, level_count)
    args = [pltpu.with_memory_space_constraint(a, pltpu.HBM) for a in args]
    *args, pair_a, pair_b, to_west, to_east, edge = call(
        pack_kernel,
        [jax.ShapeDtypeStruct(a.shape, a.dtype) for a in args]
        + [(n_pairs,) + tile] * 2
        + [(n_sent,) + tile] * 2
        + [(n_fields,) + tile],
        args,
        [pltpu.SemaphoreType.DMA((2 * n_trac + 4,))],
        pltpu.HBM,
    )
    from_west = shift(to_east, 1)
    from_east = shift(to_west, -1)
    pair_b = swap_b(pair_b)
    corner_a, corner_b = call(corner_kernel, [(n_sent,) + tile] * 2, (from_west, from_east))
    both_a = swap_a(jnp.concatenate([pair_a, corner_a]))
    pair_a, corner_a = both_a, both_a[n_pairs:]
    corner_b = swap_b(corner_b)
    outs = [tracers.shape, east_vel.shape, north_vel.shape]
    per_plane = (n_trac, lev) + tile
    near = call(
        near_kernel,
        outs + [(STEPS - 1,) + per_plane] * 2 + [(n_trac + 2,) + tile],
        (*args, pair_a),
        [(4,) + per_plane, (STEPS, 2) + per_plane, (len(COEFS), lev, 2) + tile],
    )
    near_t, near_e, near_n, past, past_adj, edge_a = near
    turned = call(
        beyond_kernel, [(2, STEPS) + per_plane, (2,) + per_plane], (args[0], args[1], past, past_adj)
    )
    *main, edge_rim = call(
        far_kernel,
        outs + [(n_fields,) + tile],
        (*args, pair_b, near_t, near_e, near_n, edge_a, *turned),
        [(4,) + per_plane] + [(STEPS, 2) + per_plane] * 2 + [(len(COEFS), lev) + tile, (2, lev) + tile],
    )
    return tuple(
        call(edge_kernel, outs, (edge, edge_rim, from_west, from_east, corner_a, corner_b, *main))
    )


def solution(mesh):
    state, flat, cell = P(None, None, "lat", "lon"), P(None, "lat", "lon"), P("lat", "lon")
    return jax.shard_map(
        adjoint,
        mesh=mesh,
        in_specs=(state, state, flat, flat, cell, cell),
        out_specs=(state, flat, flat),
        check_vma=False,
    )
```

```python
import jax
import jax.numpy as jnp
from jax import lax
from jax.experimental import pallas as pl
from jax.experimental.pallas import tpu as pltpu
from jax.sharding import PartitionSpec as P


STEPS = 4
HORIZ = 0.22
VERT = 0.05

ROWS = 8
LANES = 128
RIM = 4
SLOT = 16
F32 = jnp.float32
VMEM = 8 << 20


def iota(axis):
    return lax.broadcasted_iota(jnp.int32, (ROWS, LANES), axis)


def lane_roll(x, shift):
    shift %= LANES
    return x if shift == 0 else pltpu.roll(x, shift, 1)


def row_roll(x, shift):
    return pltpu.roll(x, shift % ROWS, 0)


def east(x):
    return lane_roll(x, -1)


def west(x):
    return lane_roll(x, 1)


def north(own, rim, last):
    a, b = row_roll(own, -1), row_roll(rim, -1)
    return jnp.where(last, b, a), jnp.where(last, a, b)


def south(own, rim, first):
    a, b = row_roll(own, 1), row_roll(rim, 1)
    return jnp.where(first, b, a), jnp.where(first, a, b)


def odd_row():
    return lax.rem(lax.axis_index("lat"), 2)


def wet_count(mask, count):
    return jnp.where(mask == 1, count, 0).astype(F32)


def edge_of(planes):
    slot = iota(1) // SLOT
    out = None
    for k, plane in enumerate(planes):
        moved = lane_roll(plane, SLOT * k + SLOT // 2)
        out = moved if out is None else jnp.where(slot == k, moved, out)
    return out


def inside_rows(rim):
    place, total = lax.axis_index("lat"), lax.axis_size("lat")
    sub = iota(0)
    keep = ((sub >= RIM) | (place < total - 1)) & ((sub < RIM) | (place > 0))
    return jnp.where(keep, rim, 0.0)


def pack_kernel(*refs):
    args, here, (pair_a, pair_b, to_west, to_east, edge, sems) = refs[:6], refs[6:12], refs[12:]
    parts = [(a.at[t], b.at[t]) for a, b in zip(args[:2], here[:2]) for t in range(a.shape[0])]
    parts += list(zip(args[2:], here[2:]))
    copies = [pltpu.make_async_copy(a, b, sems.at[i]) for i, (a, b) in enumerate(parts)]
    for copy in copies:
        copy.start()
    for copy in copies:
        copy.wait()
    trac, cot, east_vel, north_vel, mask, count = here
    n_trac, lev = trac.shape[:2]
    upper = (iota(0) // RIM) != odd_row()

    def pair(index, p, q):
        q = row_roll(q, RIM)
        pair_a[index] = jnp.where(upper, p, q)
        pair_b[index] = jnp.where(upper, q, p)

    for t in range(n_trac):
        for k in range(lev):
            pair(t * lev + k, trac[t, k], cot[t, k])
    for k in range(lev):
        pair(n_trac * lev + k, east_vel[k], north_vel[k])
    wet = wet_count(mask[...], count[...])
    pair_a[(n_trac + 1) * lev] = wet
    pair_b[(n_trac + 1) * lev] = wet

    fields = [[trac[t, k] for k in range(lev)] for t in range(n_trac)]
    fields += [[cot[t, k] for k in range(lev)] for t in range(n_trac)]
    fields += [[ref[k] for k in range(lev)] for ref in (east_vel, north_vel)]
    fields += [[wet] * lev]
    quarter = (iota(1) % SLOT) // RIM
    west_out, east_out = {}, {}
    for f, planes in enumerate(fields):
        e = edge_of(planes)
        edge[f] = e
        d, g = divmod(f, SLOT // RIM)
        if f == len(fields) - 1 and g == 0:
            west_out[d] = east_out[d] = e
            continue
        moved = lane_roll(e, RIM * g - 8)
        if g == 0:
            west_out[d] = east_out[d] = moved
        else:
            west_out[d] = jnp.where(quarter == g, moved, west_out[d])
            east_out[d] = jnp.where(quarter == g - 1, moved, east_out[d])
    for d in west_out:
        to_west[d] = west_out[d]
        to_east[d] = east_out[d]


def corner_kernel(from_west, from_east, pair_a, pair_b):
    upper = (iota(0) // RIM) != odd_row()
    for d in range(from_west.shape[0]):
        p, q = from_west[d], row_roll(from_east[d], RIM)
        pair_a[d] = jnp.where(upper, p, q)
        pair_b[d] = jnp.where(upper, q, p)


def unpair(a, b):
    from_a = (iota(0) // RIM) == odd_row()
    return jnp.where(from_a, a, b), row_roll(jnp.where(from_a, b, a), RIM)


def velocity_terms(wet, east_wet, north_wet, u, v):
    east_open, north_open = wet * east_wet, wet * north_wet
    hu, hv = 0.5 * u, 0.5 * v
    p, q = east_open * (hu + HORIZ), east_open * (HORIZ - hu)
    r, s = north_open * (hv + HORIZ), north_open * (HORIZ - hv)
    return dict(east_open=east_open, north_open=north_open, p=p, q=q, r=r, s=s, pw=west(p), qw=west(q))


def finish(c, wet, rs, ss, wet_up, wet_down):
    c["rs"], c["ss"] = rs, ss
    centre = wet - ((c["p"] + c["qw"]) + (c["r"] + ss))
    for side, other in (("up", wet_up), ("down", wet_down)):
        if other is not None:
            c[side] = (VERT * wet) * other
            centre = centre - c[side]
    c["centre"] = centre
    return c


def coefficients(wet, wet_up, wet_down, u, v):
    sub = iota(0)
    first, last = sub == 0, sub == ROWS - 1
    north_wet = north(*wet, last)
    out = [velocity_terms(wet[h], east(wet[h]), north_wet[h], u[h], v[h]) for h in range(2)]
    rs, ss = (south(out[0][x], out[1][x], first) for x in "rs")
    for h in range(2):
        finish(out[h], wet[h], rs[h], ss[h], wet_up and wet_up[h], wet_down and wet_down[h])
    return out


FORWARD = ("q", "pw", "s", "rs")
BACKWARD = ("p", "qw", "r", "ss")
COEFS = ("centre", "p", "q", "pw", "qw", "r", "s", "rs", "ss", "up", "down", "east_open", "north_open")


def combine(coef, names, x, e, w, n, s, up, down):
    out = (coef("centre") * x + coef(names[0]) * e) + (coef(names[1]) * w + coef(names[2]) * n)
    out = out + coef(names[3]) * s
    if up is not None:
        out = out + coef("up") * up
    if down is not None:
        out = out + coef("down") * down
    return out


def add(total, term):
    return term if total is None else total + term


def packed_edges(pairs, n_trac, lev):
    groups = [[pairs[i * lev + k] for k in range(lev)] for i in range(n_trac + 1)]
    return [edge_of(g) for g in groups] + [edge_of([pairs[(n_trac + 1) * lev]] * lev)]


def near_kernel(trac, cot, east_vel, north_vel, mask, count, pair_a, adj_t, adj_e, adj_n, past, past_adj, edge_a, rims, sums, coef):
    n_trac, lev = trac.shape[:2]
    sub = iota(0)
    first, last = sub == 0, sub == ROWS - 1
    for i, e in enumerate(packed_edges(pair_a, n_trac, lev)):
        edge_a[i] = e

    def rim(index):
        x = pair_a[index]
        return x, row_roll(x, RIM)

    for t in range(n_trac):
        for k in range(lev):
            rims[0, t, k], rims[2, t, k] = rim(t * lev + k)
    own_side = (sub // RIM) == odd_row()
    count_own = wet_count(mask[...], count[...])
    count_rim = jnp.where(own_side, pair_a[(n_trac + 1) * lev], 0.0)
    wet = [tuple(jnp.where(x > k, 1.0, 0.0) for x in (count_own, count_rim)) for k in range(lev)]
    for k in range(lev):
        u_rim, v_rim = rim(n_trac * lev + k)
        made = coefficients(
            wet[k],
            wet[k + 1] if k + 1 < lev else None,
            wet[k - 1] if k else None,
            (east_vel[k], u_rim),
            (north_vel[k], v_rim),
        )
        for h in range(2):
            for name, value in made[h].items():
                coef[COEFS.index(name), k, h] = value

    def states(own, buf):
        return lambda t, k: (own[t, k], rims[buf, t, k])

    def neighbours(pair):
        own, out = pair
        n, s = north(own, out, last), south(own, out, first)
        return (own, out), (east(own), east(out)), (west(own), west(out)), n, s

    def apply(get, k, t, about, names, h):
        x, e, w, n, s = about
        up = get(t, k + 1)[h] if k + 1 < lev else None
        down = get(t, k - 1)[h] if k else None
        return combine(lambda name: coef[COEFS.index(name), k, h], names, x[h], e[h], w[h], n[h], s[h], up, down)

    for step in range(STEPS):
        get = states(past.at[step - 1] if step else trac, step % 2)
        for k in range(lev):
            for t in range(n_trac):
                if step < STEPS - 1:
                    about = neighbours(get(t, k))
                    past[step, t, k] = apply(get, k, t, about, FORWARD, 0)
                    rims[(step + 1) % 2, t, k] = apply(get, k, t, about, FORWARD, 1)
                    x, e, n = about[0][0], about[1][0], about[3][0]
                else:
                    x, out = get(t, k)
                    e, n = east(x), north(x, out, last)[0]
                sums[step, 0, t, k] = x + e
                sums[step, 1, t, k] = x + n
    for done, step in enumerate(reversed(range(STEPS))):
        get = states(past_adj.at[done - 1] if done else cot, 2 + done % 2)
        for k in range(lev):
            acc_e = acc_n = None
            for t in range(n_trac):
                about = neighbours(get(t, k))
                new = apply(get, k, t, about, BACKWARD, 0)
                if step:
                    past_adj[done, t, k] = new
                    rims[2 + (done + 1) % 2, t, k] = apply(get, k, t, about, BACKWARD, 1)
                else:
                    adj_t[t, k] = new
                x, e, n = about[0][0], about[1][0], about[3][0]
                acc_e = add(acc_e, sums[step, 0, t, k] * (e - x))
                acc_n = add(acc_n, sums[step, 1, t, k] * (n - x))
            if done:
                acc_e, acc_n = acc_e + adj_e[k], acc_n + adj_n[k]
            if step == 0:
                acc_e = acc_e * (0.5 * coef[COEFS.index("east_open"), k, 0])
                acc_n = acc_n * (0.5 * coef[COEFS.index("north_open"), k, 0])
            adj_e[k] = acc_e
            adj_n[k] = acc_n


def march(steps):
    for i in range(steps):
        yield lambda part: part.backward(i)
        yield lambda part: part.forward(i)
        for step in range(steps):
            if max(step, steps - 1 - step) == i:
                yield lambda part: part.collect(step)


def beyond_kernel(trac, cot, past, past_adj, edge, from_west, from_east, beyond, beside, strip_own):
    first = iota(0) == 0
    n_trac, lev = trac.shape[:2]
    n_fields = edge.shape[0]
    for side, sent in enumerate((from_west, from_east)):
        from_side = (iota(1) % SLOT) // RIM == 1 + side
        for f in range(n_fields):
            d, g = divmod(f, SLOT // RIM)
            shift = 0 if f == n_fields - 1 and g == 0 else 8 - RIM * g
            strip_own[side, f] = jnp.where(from_side, lane_roll(sent[d], shift), edge[f])
    for i, (start, later) in enumerate(((trac, past), (cot, past_adj))):
        for t in range(n_trac):
            for k in range(lev):
                beside[i, t, k] = row_roll(start[t, k], RIM)
                for step in range(STEPS):
                    x = later[step - 1, t, k] if step else start[t, k]
                    beyond[i, step, t, k] = jnp.where(first, row_roll(x, -3), row_roll(x, 3))


class Far:
    def __init__(self, args, pair_b, beyond, beside, state, sums, slopes, coef, acc):
        self.slopes, self.started = slopes, False
        self.trac, self.cot, east_vel, north_vel, mask, count = args
        self.beyond, self.state, self.sums, self.coef, self.acc = beyond, state, sums, coef, acc
        n_trac, lev = self.n_trac, self.lev = self.trac.shape[:2]
        sub = iota(0)
        self.first, self.last = sub == 0, sub == ROWS - 1
        self.rim = (sub // RIM) == odd_row()

        def both(index, p, q):
            x = pair_b[index]
            return jnp.where(self.rim, row_roll(x, RIM), p), jnp.where(self.rim, x, q)

        for t in range(n_trac):
            for k in range(lev):
                state[0, t, k], state[2, t, k] = both(t * lev + k, beside[0, t, k], beside[1, t, k])
        place = lax.axis_index("lat")
        outside = (place == 0) | (place == lax.axis_size("lat") - 1)
        count_own = wet_count(mask[...], count[...])
        count_rim = row_roll(pair_b[(n_trac + 1) * lev], RIM)
        count_far = self.join(jnp.where(outside, jnp.zeros_like(count_rim), count_rim), count_own)
        own = [jnp.where(count_own > k, 1.0, 0.0) for k in range(lev)]
        far = [jnp.where(count_far > k, 1.0, 0.0) for k in range(lev)]
        for k in range(lev):
            u, v = both(n_trac * lev + k, row_roll(east_vel[k], RIM), row_roll(north_vel[k], RIM))
            beyond = velocity_terms(own[k], own[k], row_roll(own[k], -1), north_vel[k], north_vel[k])
            made = velocity_terms(far[k], east(far[k]), self.north(far[k], own[k]), u, v)
            rs, ss = (self.south(made[x], beyond[x]) for x in "rs")
            finish(made, far[k], rs, ss, far[k + 1] if k + 1 < lev else None, far[k - 1] if k else None)
            for name, value in made.items():
                coef[COEFS.index(name), k] = value

    def join(self, rim, own):
        return jnp.where(self.rim, rim, row_roll(own, RIM))

    def north(self, x, beyond):
        return jnp.where(self.last, row_roll(beyond, 3), row_roll(x, -1))

    def south(self, x, beyond):
        return jnp.where(self.first, row_roll(beyond, -3), row_roll(x, 1))

    def next_row(self, x, beyond):
        return jnp.where(self.last, beyond, row_roll(x, -1))

    def row_before(self, x, beyond):
        return jnp.where(self.first, beyond, row_roll(x, 1))

    def apply(self, buf, t, k, about, names):
        up = self.state[buf, t, k + 1] if k + 1 < self.lev else None
        down = self.state[buf, t, k - 1] if k else None
        return combine(lambda name: self.coef[COEFS.index(name), k], names, *about, up, down)

    def forward(self, step):
        src, dst = step % 2, (step + 1) % 2
        for k in range(self.lev):
            for t in range(self.n_trac):
                x, beyond = self.state[src, t, k], self.beyond[0, step, t, k]
                e, n = east(x), self.next_row(x, beyond)
                self.sums[step, 0, t, k] = x + e
                self.sums[step, 1, t, k] = x + n
                if step < STEPS - 1:
                    about = x, e, west(x), n, self.row_before(x, beyond)
                    self.state[dst, t, k] = self.apply(src, t, k, about, FORWARD)

    def backward(self, done):
        step = STEPS - 1 - done
        src, dst = 2 + done % 2, 2 + (done + 1) % 2
        for k in range(self.lev):
            for t in range(self.n_trac):
                x, beyond = self.state[src, t, k], self.beyond[1, done, t, k]
                e, n = east(x), self.next_row(x, beyond)
                about = x, e, west(x), n, self.row_before(x, beyond)
                self.state[dst, t, k] = self.apply(src, t, k, about, BACKWARD)
                self.slopes[step, 0, t, k] = e - x
                self.slopes[step, 1, t, k] = n - x

    def collect(self, step):
        for k in range(self.lev):
            for i in range(2):
                total = self.acc[i, k] if self.started else None
                for t in range(self.n_trac):
                    total = add(total, self.sums[step, i, t, k] * self.slopes[step, i, t, k])
                self.acc[i, k] = total
        self.started = True

    def merged(self, t, k, near):
        return jnp.where(self.rim, row_roll(self.state[2 + STEPS % 2, t, k], RIM), near)

    def merged_gradient(self, i, k, near):
        opened = self.coef[COEFS.index(("east_open", "north_open")[i]), k]
        return jnp.where(self.rim, row_roll(self.acc[i, k] * (0.5 * opened), RIM), near)


class Strip:
    def __init__(self, side, n_trac, lev, strip_own, rims, corners):
        self.n_trac = n_trac
        n_fields = strip_own.shape[1]
        sub, lane = iota(0), iota(1)
        self.first, self.last = sub == 0, sub == ROWS - 1
        level = lane // SLOT
        from_side = (lane % SLOT) // RIM == 1 + side

        def field(f):
            d, g = divmod(f, SLOT // RIM)
            shift = 0 if f == n_fields - 1 and g == 0 else 8 - RIM * g
            own = strip_own[side, f]
            rim = jnp.where(from_side, lane_roll(corners[d], shift), rims[f])
            return own, rim

        own, rim = field(n_fields - 1)
        levels = level.astype(F32)
        wet = tuple(jnp.where(x > levels, 1.0, 0.0) for x in (own, inside_rows(rim)))
        up = tuple(jnp.where(level < lev - 1, lane_roll(x, -SLOT), 0.0) for x in wet)
        down = tuple(jnp.where(level > 0, lane_roll(x, SLOT), 0.0) for x in wet)
        self.made = coefficients(wet, up, down, field(2 * n_trac), field(2 * n_trac + 1))
        self.state = [field(t) for t in range(n_trac)]
        self.lam = [field(n_trac + t) for t in range(n_trac)]
        self.sums, self.slopes, self.acc_e, self.acc_n = [], {}, None, None

    def near(self, x):
        n, s = north(*x, self.last), south(*x, self.first)
        return x, tuple(map(east, x)), tuple(map(west, x)), n, s

    def apply(self, about, names, halves):
        x, e, w, n, s = about
        return tuple(
            combine(self.made[h].__getitem__, names, x[h], e[h], w[h], n[h], s[h], lane_roll(x[h], -SLOT), lane_roll(x[h], SLOT))
            for h in halves
        )

    def forward(self, step):
        about = [self.near(x) for x in self.state]
        self.sums.append([(a[0][0] + a[1][0], a[0][0] + a[3][0]) for a in about])
        if step < STEPS - 1:
            self.state = [self.apply(a, FORWARD, (0, 1)) for a in about]

    def backward(self, done):
        step = STEPS - 1 - done
        about = [self.near(x) for x in self.lam]
        self.slopes[step] = [(a[1][0] - a[0][0], a[3][0] - a[0][0]) for a in about]
        self.lam = [self.apply(a, BACKWARD, (0, 1) if step else (0,)) for a in about]

    def collect(self, step):
        for (sum_e, sum_n), (slope_e, slope_n) in zip(self.sums[step], self.slopes[step]):
            self.acc_e = add(self.acc_e, sum_e * slope_e)
            self.acc_n = add(self.acc_n, sum_n * slope_n)

    def gradients(self):
        own = self.made[0]
        return self.acc_e * (0.5 * own["east_open"]), self.acc_n * (0.5 * own["north_open"])


def far_kernel(*refs):
    args, refs = refs[:6], refs[6:]
    pair_b, near_t, near_e, near_n, edge_a, beyond, beside = refs[:7]
    adj_t, adj_e, adj_n, edge_rim, state, sums, slopes, coef, acc = refs[7:]
    n_trac, lev = near_t.shape[:2]

    for i, b in enumerate(packed_edges(pair_b, n_trac, lev)):
        p, q = unpair(edge_a[i], b)
        if i < n_trac:
            edge_rim[i], edge_rim[n_trac + i] = p, q
        elif i == n_trac:
            edge_rim[2 * n_trac], edge_rim[2 * n_trac + 1] = p, q
        else:
            edge_rim[2 * n_trac + 2] = p
    far = Far(args, pair_b, beyond, beside, state, sums, slopes, coef, acc)
    for part in march(STEPS):
        part(far)
    for k in range(lev):
        for t in range(n_trac):
            adj_t[t, k] = far.merged(t, k, near_t[t, k])
        adj_e[k] = far.merged_gradient(0, k, near_e[k])
        adj_n[k] = far.merged_gradient(1, k, near_n[k])


def edge_kernel(strip_own, edge_rim, corner_a, corner_b, main_t, main_e, main_n, adj_t, adj_e, adj_n):
    n_trac, lev = main_t.shape[:2]
    corners = [unpair(corner_a[d], corner_b[d]) for d in range(corner_a.shape[0])]
    strips = [Strip(side, n_trac, lev, strip_own, edge_rim, [c[side] for c in corners]) for side in range(2)]
    for part in march(STEPS):
        for strip in strips:
            part(strip)

    lane = iota(1)
    at_west = (lane % SLOT) // RIM >= 2
    margin = (lane < RIM) | (lane >= LANES - RIM)

    def put(ref, index, k, both, main):
        ref[index] = jnp.where(margin, lane_roll(both, -(SLOT * k + SLOT // 2)), main[index])

    for t in range(n_trac):
        both = jnp.where(at_west, strips[0].lam[t][0], strips[1].lam[t][0])
        for k in range(lev):
            put(adj_t, (t, k), k, both, main_t)
    for ref, main, *sides in zip((adj_e, adj_n), (main_e, main_n), *(s.gradients() for s in strips)):
        both = jnp.where(at_west, *sides)
        for k in range(lev):
            put(ref, (k,), k, both, main)


def call(body, outs, args, scratch=(), space=pltpu.VMEM):
    shapes = [s if hasattr(s, "dtype") else jax.ShapeDtypeStruct(s, F32) for s in outs]
    return pl.pallas_call(
        body,
        out_shape=shapes,
        in_specs=[pl.BlockSpec(memory_space=space)] * len(args),
        out_specs=[pl.BlockSpec(memory_space=pltpu.VMEM)] * len(outs),
        scratch_shapes=[pltpu.VMEM(s, F32) if isinstance(s, tuple) else s for s in scratch],
        compiler_params=pltpu.CompilerParams(vmem_limit_bytes=VMEM),
    )(*args)


def adjoint(tracers, cotangent, east_vel, north_vel, sea_mask, level_count):
    n_trac, lev, rows, cols = tracers.shape
    assert (rows, cols, lev * SLOT) == (ROWS, LANES, LANES)
    n_lon, n_lat = lax.axis_size("lon"), lax.axis_size("lat")
    assert n_lat % 2 == 0
    n_pairs = (n_trac + 1) * lev + 1
    n_fields = 2 * n_trac + 3
    n_sent = -(-n_fields * RIM // SLOT)
    tile = (rows, cols)

    def swap_a(x):
        return lax.ppermute(x, "lat", [(j, j ^ 1) for j in range(n_lat)])

    def swap_b(x):
        pairs = []
        for i in range(n_lon):
            for j in range(n_lat):
                end = j in (0, n_lat - 1)
                to = (i ^ 1, j) if end else (i, ((j + 1) ^ 1) - 1)
                pairs.append((i * n_lat + j, to[0] * n_lat + to[1]))
        return lax.ppermute(x, ("lon", "lat"), pairs)

    def shift(x, by):
        return lax.ppermute(x, "lon", [(i, (i + by) % n_lon) for i in range(n_lon)])

    args = (tracers, cotangent, east_vel, north_vel, sea_mask, level_count)
    args = [pltpu.with_memory_space_constraint(a, pltpu.HBM) for a in args]
    *args, pair_a, pair_b, to_west, to_east, edge = call(
        pack_kernel,
        [jax.ShapeDtypeStruct(a.shape, a.dtype) for a in args]
        + [(n_pairs,) + tile] * 2
        + [(n_sent,) + tile] * 2
        + [(n_fields,) + tile],
        args,
        [pltpu.SemaphoreType.DMA((2 * n_trac + 4,))],
        pltpu.HBM,
    )
    from_west = shift(to_east, 1)
    from_east = shift(to_west, -1)
    pair_b = swap_b(pair_b)
    corner_a, corner_b = call(corner_kernel, [(n_sent,) + tile] * 2, (from_west, from_east))
    both_a = swap_a(jnp.concatenate([pair_a, corner_a]))
    pair_a, corner_a = both_a, both_a[n_pairs:]
    corner_b = swap_b(corner_b)
    outs = [tracers.shape, east_vel.shape, north_vel.shape]
    per_plane = (n_trac, lev) + tile
    near = call(
        near_kernel,
        outs + [(STEPS - 1,) + per_plane] * 2 + [(n_trac + 2,) + tile],
        (*args, pair_a),
        [(4,) + per_plane, (STEPS, 2) + per_plane, (len(COEFS), lev, 2) + tile],
    )
    near_t, near_e, near_n, past, past_adj, edge_a = near
    *turned, strip_own = call(
        beyond_kernel,
        [(2, STEPS) + per_plane, (2,) + per_plane, (2, n_fields) + tile],
        (args[0], args[1], past, past_adj, edge, from_west, from_east),
    )
    *main, edge_rim = call(
        far_kernel,
        outs + [(n_fields,) + tile],
        (*args, pair_b, near_t, near_e, near_n, edge_a, *turned),
        [(4,) + per_plane] + [(STEPS, 2) + per_plane] * 2 + [(len(COEFS), lev) + tile, (2, lev) + tile],
    )
    return tuple(
        call(edge_kernel, outs, (strip_own, edge_rim, corner_a, corner_b, *main))
    )


def solution(mesh):
    state, flat, cell = P(None, None, "lat", "lon"), P(None, "lat", "lon"), P("lat", "lon")
    return jax.shard_map(
        adjoint,
        mesh=mesh,
        in_specs=(state, state, flat, flat, cell, cell),
        out_specs=(state, flat, flat),
        check_vma=False,
    )
```
